32 devices in a mesh: leaf: 8 (over z, core), rep: 4 (over y, x).
Axes of the slice: x: 2, y: 2, z: 4, core: 2. Of those that a mesh axis runs over, the one named last changes fastest.
Arguments:
- curve_coordinates: float32 [2, 65536], P(None, 'leaf'), may hold values from -1.25 to 1.25, as said below
- weighted_density: float32 [65536], P('leaf'), may hold values from 0.02 to 0.2
- random_test_matrix: float32 [128, 65536], P('rep', 'leaf'), may hold values from -6 to 6
- sketch_matrix: float32 [128, 65536], P('rep', 'leaf'), may hold values from -12 to 12
Outputs:
- leaf_basis: float32 [128, 65536], P('rep', 'leaf')
- top_basis: float32 [8, 128, 256], P('leaf', 'rep')
The draws below stay inside these ranges and needn't reach their ends.
Inputs may be any that keep to these rules, and one draw needn't show every extreme that they name: `curve_coordinates`: the points are in order along one closed smooth curve, one point in each of 65536 equal parameter cells.
All inputs are finite; a program needn't handle non-finite values.
Results may differ from the reference program's by a relative error of at most 0.00035.
Values sent between devices are 32-bit elements; how exact they have to be, the bound alone decides.
A program may use at most 64 MiB of HBM per device.

```python
import math
import jax
import jax.numpy as jnp
from jax import lax

NODES_PER_CELL = 512
S = 128
LEAF_LEVELS = 4
CROSS = 3
CURVE_NODE_NUM = 65536


def draw_curve_coordinates(key, part):
    position = jnp.arange(CURVE_NODE_NUM, dtype=jnp.float32)
    jitter = jax.random.uniform(key, (CURVE_NODE_NUM,), jnp.float32, -0.3, 0.3)
    angle_rad = 2.0 * math.pi * (position + 0.5 + jitter) / CURVE_NODE_NUM
    radius = 1.0 + 0.2 * jnp.cos(5.0 * angle_rad)
    return jnp.stack([radius * jnp.cos(angle_rad), radius * jnp.sin(angle_rad)])


def steps_of(own_key, shape, shards, smallest, top_value):
    loudness = 1.0
    for axis_at, parts in shards:
        steps = jax.random.uniform(jax.random.fold_in(jax.random.fold_in(own_key, 6), axis_at), (parts,), jnp.float32, smallest / len(shards), top_value / len(shards))
        loudness = loudness * jnp.repeat(jnp.exp(steps), shape[axis_at] // parts).reshape((-1,) + (1,) * (len(shape) - 1 - axis_at))
    return loudness


def bell_draw(rng, dims, deviation, reach, split=(), held_as=jnp.bfloat16):
    result = deviation * jax.random.normal(rng, dims, jnp.float32)
    if split:
        result = result * steps_of(rng, dims, split, -0.22, 0.18)
    return jnp.clip(result, -reach, reach).astype(held_as)


def setup_inputs(seed: int = 0) -> dict:
    streams_of = jax.random.split(jax.random.key(seed), 5)
    curve_coordinates = draw_curve_coordinates(jax.random.fold_in(streams_of[4], 71), 0)
    weighted_density = jnp.clip(jnp.exp(math.log(0.2) - 2.3025851 * jax.random.uniform(streams_of[1], (CURVE_NODE_NUM,), jnp.float32) ** steps_of(streams_of[1], (CURVE_NODE_NUM,), ((0, 8),), -0.2, 0.2)), 0.02, 0.2)
    random_test_matrix = bell_draw(streams_of[2], (S, CURVE_NODE_NUM), 1.0, 6.0, ((0, 4), (1, 8)), jnp.float32)
    sketch_matrix = bell_draw(streams_of[3], (S, CURVE_NODE_NUM), 2.0, 12.0, ((0, 4), (1, 8)), jnp.float32)
    return {"curve_coordinates": curve_coordinates, "weighted_density": weighted_density, "random_test_matrix": random_test_matrix, "sketch_matrix": sketch_matrix}


grouping = 4

def distances(targets, sources):
    delta_x = targets[0][:, None] - sources[0][None, :]
    delta_y = targets[1][:, None] - sources[1][None, :]
    return delta_x * delta_x + delta_y * delta_y

def near_field(window, blocks):
    span = window.shape[2]
    height = window.shape[1]
    row_ids = lax.broadcasted_iota(jnp.int32, (span, 3 * span), 0)
    col_ids = lax.broadcasted_iota(jnp.int32, (span, 3 * span), 1)
    same = row_ids + span == col_ids
    results = []
    for offset in range(blocks):
        sources = window[offset:offset + 3].transpose(1, 0, 2).reshape(height, 3 * span)
        targets = window[offset + 1, :2]
        squared = distances(targets, sources[:2])
        guarded = jnp.where(same, 1.0, squared)
        potential = jnp.log(guarded) * (-0.25 / math.pi)
        self_term = (1.0 - jnp.log(0.5 * sources[2])) * (0.5 / math.pi)
        matrix = jnp.where(same, self_term[None, :], potential) * sources[2][None, :]
        results.append(jnp.einsum('cj,ij->ci', sources[3:], matrix, precision=lax.Precision.HIGHEST))
    return jnp.stack(results)

def couple(skel_rows, skel_cols):

    def single(rows, cols):
        return jnp.log(distances(rows[:2], cols[:2])) * (-0.25 / math.pi) * cols[2][None, :]
    return jax.vmap(single)(skel_rows, skel_cols)

def assemble(sample_hat, probe_hat, skeleton):
    upper_y, lower_y = (sample_hat[0::2], sample_hat[1::2])
    upper_w, lower_w = (probe_hat[0::2], probe_hat[1::2])
    upper_s, lower_s = (skeleton[0::2], skeleton[1::2])
    cross_ab = couple(upper_s, lower_s)
    cross_ba = couple(lower_s, upper_s)
    top_rows = upper_y - jnp.einsum('nct,nst->ncs', lower_w, cross_ab, precision=lax.Precision.HIGHEST)
    bottom_rows = lower_y - jnp.einsum('nct,nst->ncs', upper_w, cross_ba, precision=lax.Precision.HIGHEST)
    off_diag = jnp.concatenate([top_rows, bottom_rows], 2)
    joined_y = jnp.concatenate([upper_y, lower_y], 2)
    joined_w = jnp.concatenate([upper_w, lower_w], 2)
    joined_s = jnp.concatenate([upper_s, lower_s], 2)[:, :, ::2]
    parent_s = jnp.concatenate([joined_s[:, :2], 2.0 * joined_s[:, 2:]], 1)
    return (off_diag, joined_y, joined_w, parent_s)

def project(basis_rows, stacked):
    return jnp.einsum('nsm,ncm->ncs', basis_rows, stacked, precision=lax.Precision.HIGHEST)

def orthonormal(off_diag):
    gram = jnp.einsum('nsm,ntm->nst', off_diag, off_diag, precision=lax.Precision.HIGHEST)
    factor = jnp.linalg.cholesky(gram)
    order = gram.shape[1]
    identity = jnp.eye(order, dtype=gram.dtype)
    inverse = jax.vmap(lambda low: jax.scipy.linalg.solve_triangular(low, identity, lower=True))(factor)
    return jnp.einsum('nst,ntm->nsm', inverse, off_diag, precision=lax.Precision.HIGHEST)

def reference(curve_coordinates, weighted_density, random_test_matrix, sketch_matrix):
    total = curve_coordinates.shape[1]
    number_finest_cells = total // NODES_PER_CELL
    step_width = NODES_PER_CELL // S
    finest_cell_coordinates = curve_coordinates.reshape(2, number_finest_cells, NODES_PER_CELL).transpose(1, 0, 2)
    finest_cell_weights = weighted_density.reshape(number_finest_cells, 1, NODES_PER_CELL)
    finest_cell_random_test = random_test_matrix.reshape(S, number_finest_cells, NODES_PER_CELL).transpose(1, 0, 2)
    leaf_y = sketch_matrix.reshape(S, number_finest_cells, NODES_PER_CELL).transpose(1, 0, 2)
    scratch_buffer = jnp.concatenate([finest_cell_coordinates, finest_cell_weights, finest_cell_random_test], 1)
    padded_rows = jnp.concatenate([scratch_buffer[-1:], scratch_buffer, scratch_buffer[:1]], 0)

    def block_near(block_index):
        window = lax.dynamic_slice_in_dim(padded_rows, block_index * grouping, grouping + 2, 0)
        return near_field(window, grouping)
    near = lax.map(block_near, jnp.arange(number_finest_cells // grouping, dtype=jnp.int32))
    near = near.reshape(number_finest_cells, S, NODES_PER_CELL)
    off_diag = leaf_y - near
    basis_rows = orthonormal(off_diag)
    leaf_basis = basis_rows.transpose(1, 0, 2).reshape(S, total) * math.sqrt(NODES_PER_CELL)
    sample_hat = project(basis_rows, leaf_y)
    probe_hat = project(basis_rows, finest_cell_random_test)
    skeleton_unpruned = scratch_buffer[:, :3, ::step_width]
    skeleton = jnp.concatenate([skeleton_unpruned[:, :2], step_width * skeleton_unpruned[:, 2:]], 1)
    for level in range(LEAF_LEVELS + CROSS):
        off_diag, joined_y, joined_w, skeleton = assemble(sample_hat, probe_hat, skeleton)
        basis_rows = orthonormal(off_diag)
        sample_hat = project(basis_rows, joined_y)
        probe_hat = project(basis_rows, joined_w)
    top_basis = jnp.repeat(basis_rows, 2 ** CROSS, axis=0) * math.sqrt(2 * S)
    return (leaf_basis, top_basis)
```

```python
import functools
import math

import jax
import jax.numpy as jnp
from jax import lax
from jax.experimental import pallas as pl
from jax.experimental.pallas import tpu as pltpu
from jax.sharding import PartitionSpec as P

NODES_PER_CELL = 512
S = 128
LEAF_LEVELS = 4
CROSS = 3
PANEL = 32
GROUP = 8
HIGHEST = lax.Precision.HIGHEST
LOG_SCALE = -0.25 / math.pi
VMEM_LIMIT = 60000 * 1024


def matmul(a, b, contract=(1, 0)):
    return lax.dot_general(
        a,
        b,
        (((contract[0],), (contract[1],)), ((), ())),
        precision=HIGHEST,
        preferred_element_type=jnp.float32,
    )


def split_bf16(value):
    high = value.astype(jnp.bfloat16)
    return high, (value - high.astype(jnp.float32)).astype(jnp.bfloat16)


def lane_cast(value, k):
    return jnp.broadcast_to(value[:, k : k + 1], value.shape)


def row_cast(value, j):
    return jnp.broadcast_to(value[j : j + 1, :], (8, value.shape[1]))


def inverse_factor(grams, work_ref):
    order = grams[0].shape[0]
    count = len(grams)
    for i, gram in enumerate(grams):
        work_ref[i] = gram
    lane = lax.broadcasted_iota(jnp.int32, (8, order), 1)
    sub = lax.broadcasted_iota(jnp.int32, (8, order), 0)
    for start in range(0, order, PANEL):
        tiles = PANEL // 8
        stop = start + PANEL
        panels = [
            [work_ref[i, start + 8 * v : start + 8 * v + 8, :] for v in range(tiles)]
            for i in range(count)
        ]
        for k in range(start, stop, GROUP):
            first = (k - start) // 8
            offset = k % 8
            in_group = (lane >= k) & (lane < k + GROUP)
            below = sub > offset + GROUP - 1
            for i in range(count):
                tile = panels[i]
                rows = [row_cast(tile[first], offset + j) for j in range(GROUP)]
                pivot = {
                    (j, l): lane_cast(rows[j], k + l)
                    for j in range(GROUP)
                    for l in range(j, GROUP)
                }
                live = [v for v in range(first, tiles) if v > first or offset + GROUP < 8]
                column = {v: [lane_cast(tile[v], k + l) for l in range(GROUP)] for v in live}
                if first in column:
                    column[first] = [jnp.where(below, c, 0.0) for c in column[first]]
                rows = [
                    jnp.where(in_group, jnp.where(lane == k + j, 1.0, 0.0), rows[j])
                    for j in range(GROUP)
                ]
                for v in range(first, tiles):
                    tile[v] = jnp.where(in_group, 0.0, tile[v])
                scaled = []
                for j in range(GROUP):
                    diagonal = pivot[j, j]
                    reciprocal = 1.0 / diagonal
                    for l in range(j + 1, GROUP):
                        factor = pivot[j, l] * reciprocal
                        rows[l] = rows[l] - factor * rows[j]
                        for q in range(l, GROUP):
                            pivot[l, q] = pivot[l, q] - factor * pivot[j, q]
                    for v in live:
                        multiplier = column[v][j] * reciprocal
                        for l in range(j + 1, GROUP):
                            column[v][l] = column[v][l] - multiplier * pivot[j, l]
                        tile[v] = tile[v] - multiplier * rows[j]
                    root = lax.rsqrt(diagonal)
                    root = root * (1.5 - 0.5 * diagonal * root * root)
                    scaled.append(rows[j] * root)
                for j in range(GROUP):
                    tile[first] = jnp.where(sub == offset + j, scaled[j], tile[first])
        for i in range(count):
            panel = jnp.concatenate(panels[i], 0)
            lanes = lax.broadcasted_iota(jnp.int32, panel.shape, 1)
            places = lax.broadcasted_iota(jnp.int32, panel.shape, 0) + start
            above = lanes > places
            work_ref[i, start:stop, :] = jnp.where(above, 0.0, panel)
            if stop < order:
                kept = jnp.where(above & (lanes < stop), 0.0, panel)
                rest = work_ref[i, stop:, :]
                rest_lanes = lax.broadcasted_iota(jnp.int32, rest.shape, 1)
                cleared = jnp.where((rest_lanes >= start) & (rest_lanes < stop), 0.0, rest)
                work_ref[i, stop:, :] = cleared - matmul(panel.T[stop:, :], kept)


def peer_of(stride):
    ranks = lax.axis_size("rep")
    place = lax.axis_index("leaf") * ranks + lax.axis_index("rep")
    peer = place + stride * (1 - 2 * ((place // stride) % 2))
    return (peer // ranks, peer % ranks)


def select_lanes(block, stride):
    source = block.shape[1]
    target = source // stride
    take = lax.broadcasted_iota(jnp.int32, (source, target), 0) == stride * lax.broadcasted_iota(
        jnp.int32, (source, target), 1
    )
    return matmul(block, jnp.where(take, 1.0, 0.0))


def log_kernel(source_cols, target_rows):
    delta_x = source_cols[:, 0:1] - target_rows[0:1, :]
    delta_y = source_cols[:, 1:2] - target_rows[1:2, :]
    return jnp.log(delta_x * delta_x + delta_y * delta_y) * LOG_SCALE


def off_diagonal(y_a, y_b, w_a, w_b, rows_a, rows_b):
    potential = log_kernel(rows_b.T, rows_a)
    z_a = y_a - matmul(w_b * rows_b[2:3, :], potential)
    z_b = y_b - matmul(w_a * rows_a[2:3, :], potential, (1, 1))
    return z_a, z_b


def pair_products(z_a, z_b, y_a, y_b, w_a, w_b):
    return [
        matmul(a, z_a, (1, 1)) + matmul(b, z_b, (1, 1))
        for a, b in ((z_a, z_b), (y_a, y_b), (w_a, w_b))
    ]


def tree_kernel(
    leaf_count,
    coords_ref,
    density_ref,
    probe_ref,
    sketch_ref,
    basis_out,
    top_out,
    probe_win,
    sketch_win,
    z_ref,
    basis_ref,
    points_ref,
    window_ref,
    window_cols,
    halo_xy,
    halo_w,
    high_ref,
    low_ref,
    level_refs,
    gathered,
    rows_mine,
    rows_other,
    mine_ref,
    other_ref,
    hats_ref,
    leaf_inverse,
    work_ref,
    probe_sem,
    sketch_sem,
    out_sem,
    edge_sem,
    point_sem,
    point_out_sem,
    gather_sem,
    send_sem,
    recv_sem,
    basis_sem,
    basis_out_sem,
):
    span = NODES_PER_CELL
    ranks, leaves = lax.axis_size("rep"), lax.axis_size("leaf")
    rank, position = lax.axis_index("rep"), lax.axis_index("leaf")
    columns, width = probe_ref.shape
    total_leaves = width // span
    chunk = leaf_count * span
    local_levels = leaf_count.bit_length() - 1
    rep_levels = LEAF_LEVELS - local_levels
    merges = rep_levels + CROSS
    family = 1 << CROSS
    mesh_id = pl.DeviceIdType.MESH
    after = lax.rem(position + 1, leaves)
    before = lax.rem(position + leaves - 1, leaves)
    barrier = pltpu.get_barrier_semaphore()

    def signal(leaf, rep):
        pl.semaphore_signal(barrier, inc=1, device_id=(leaf, rep), device_id_type=mesh_id)

    @pl.when(rank == 0)
    def _():
        for k in range(ranks):
            signal(before, k)

    @pl.when(rank == ranks - 1)
    def _():
        for k in range(ranks):
            signal(after, k)

    signal(after, rank)
    signal(before, rank)
    for j in range(1, family):
        signal(position ^ j, rank)
    for k in range(1, ranks):
        signal(position, rank ^ k)
    pl.semaphore_wait(barrier, 2 + 2 + (family - 1) + (ranks - 1))

    def remote(src, dst, sent, arrived, leaf, rep):
        return pltpu.make_async_remote_copy(
            src_ref=src,
            dst_ref=dst,
            send_sem=sent,
            recv_sem=arrived,
            device_id=(leaf, rep),
            device_id_type=mesh_id,
        )

    point_copies = []
    for side, leaf, start in ((0, after, width - span), (1, before, 0)):
        for i, (src, dst) in enumerate(((coords_ref, halo_xy), (density_ref, halo_w))):
            point_copies.append(
                remote(
                    src.at[:, pl.ds(start, span)],
                    dst.at[side],
                    point_out_sem.at[2 * side + i],
                    point_sem.at[2 * side + i],
                    leaf,
                    rank,
                )
            )
    for copy in point_copies:
        copy.start()

    own_rows = pl.ds(pl.multiple_of(rank * columns, 8), columns)

    def probe_copy(k, piece, local):
        rep = rank ^ k
        index = rep * leaf_count + piece - 1
        leaf, source = position, index
        if piece == 0:
            leaf = jnp.where(rep == 0, after, position)
            source = jnp.where(rep == 0, total_leaves - 1, index)
        elif piece == leaf_count + 1:
            leaf = jnp.where(rep == ranks - 1, before, position)
            source = jnp.where(rep == ranks - 1, 0, index)
        src = probe_ref.at[:, pl.ds(pl.multiple_of(source * span, span), span)]
        dst = probe_win.at[own_rows, pl.ds(piece * span, span)]
        if local:
            return pltpu.make_async_copy(src, dst, probe_sem.at[piece])
        sent = out_sem.at[k] if k else edge_sem.at[0 if piece == 0 else 1]
        return remote(src, dst, sent, probe_sem.at[piece], leaf, rep)

    def sketch_copy(k, piece):
        rep = rank ^ k
        source = pl.multiple_of((rep * leaf_count + piece) * span, span)
        src = sketch_ref.at[:, pl.ds(source, span)]
        dst = sketch_win.at[own_rows, pl.ds(piece * span, span)]
        if k == 0:
            return pltpu.make_async_copy(src, dst, sketch_sem.at[piece])
        return remote(src, dst, out_sem.at[k], sketch_sem.at[piece], position, rep)

    def start_probe(piece):
        for k in range(1, ranks):
            probe_copy(k, piece, False).start()
        if piece == 0 or piece == leaf_count + 1:
            edge = rank == (0 if piece == 0 else ranks - 1)

            @pl.when(edge)
            def _():
                probe_copy(0, piece, False).start()

            @pl.when(jnp.logical_not(edge))
            def _():
                probe_copy(0, piece, True).start()

        else:
            probe_copy(0, piece, True).start()

    def start_sketch(piece):
        for k in range(1, ranks):
            sketch_copy(k, piece).start()
        sketch_copy(0, piece).start()

    batch = min(2, leaf_count)
    sent_pieces = 0
    for first in range(0, leaf_count, batch):
        while sent_pieces < first + batch + 2:
            start_probe(sent_pieces)
            sent_pieces += 1
        for piece in range(first, first + batch):
            start_sketch(piece)

    points_ref[...] = jnp.zeros_like(points_ref)
    points_ref[0:2, :] = coords_ref[...]
    points_ref[2:3, :] = density_ref[...]
    blocks = [points_ref[:, t * span : (t + 1) * span] for t in range(total_leaves)]
    nodes = select_lanes(jnp.concatenate(blocks, 0), span // S)
    level_refs[0] = nodes
    for level in range(1, LEAF_LEVELS + 1):
        count = total_leaves >> level
        joined = [
            jnp.concatenate([nodes[16 * i : 16 * i + 8], nodes[16 * i + 8 : 16 * i + 16]], 1)
            for i in range(count)
        ]
        nodes = select_lanes(jnp.concatenate(joined, 0), 2)
        level_refs[level, : 8 * count] = nodes
    place = lax.rem(position, family)
    gathered[place] = nodes

    def gather_copy(j):
        return remote(
            gathered.at[place],
            gathered.at[place],
            gather_sem.at[0],
            gather_sem.at[1],
            position ^ j,
            rank,
        )

    for j in range(1, family):
        gather_copy(j).start()

    def skeleton(level, node):
        rows = level_refs[level, pl.ds(pl.multiple_of(node * 8, 8), 8), :]
        scaled = lax.broadcasted_iota(jnp.int32, rows.shape, 0) == 2
        return jnp.where(scaled, rows * ((span // S) << level), rows)

    for level in range(rep_levels):
        node = rank >> level
        rows_mine[level] = skeleton(local_levels + level, node)
        rows_other[level] = skeleton(local_levels + level, node ^ 1)

    for copy in point_copies:
        copy.wait()
    base = rank * chunk
    window_ref[:, span : span + chunk] = points_ref[:, pl.ds(pl.multiple_of(base, span), chunk)]
    for side in range(2):
        at = 0 if side == 0 else span + chunk
        edge = rank == (0 if side == 0 else ranks - 1)
        inner = base - span if side == 0 else base + chunk
        inner = jnp.where(edge, 0, inner)
        own = points_ref[:, pl.ds(pl.multiple_of(inner, span), span)]
        window_ref[:, at : at + span] = own
        window_ref[0:2, at : at + span] = jnp.where(edge, halo_xy[side], own[0:2])
        window_ref[2:3, at : at + span] = jnp.where(edge, halo_w[side], own[2:3])
    for t in range(leaf_count + 2):
        window_cols[t * span : (t + 1) * span, :] = window_ref[:, t * span : (t + 1) * span].T

    def fill(i, carry):
        own = i > leaf_count
        source = jnp.where(own, i - leaf_count, i)
        target = jnp.where(own, i - leaf_count, i + 1)
        cols = window_cols[pl.ds(pl.multiple_of(source * span, span), span), :]
        rows = window_ref[:, pl.ds(pl.multiple_of(target * span, span), span)]
        delta_x = cols[:, 0:1] - rows[0:1, :]
        delta_y = cols[:, 1:2] - rows[1:2, :]
        squared = delta_x * delta_x + delta_y * delta_y
        same = lax.broadcasted_iota(jnp.int32, (span, span), 0) == lax.broadcasted_iota(
            jnp.int32, (span, span), 1
        )
        squared = jnp.where(same & own, 1.0, squared)
        high, low = split_bf16(jnp.log(squared))
        high_ref[i] = high
        low_ref[i] = low
        return carry

    lax.fori_loop(0, 2 * leaf_count + 1, fill, 0)

    for copy_of in range(1):
        seven = gathered.at[pl.ds(0, family - 1)]
        pltpu.make_async_copy(seven, seven, gather_sem.at[1]).wait()
        pltpu.make_async_copy(seven, seven, gather_sem.at[0]).wait()
    for level in range(CROSS):
        lanes = S >> level
        node = place >> level
        for target_ref, which in ((rows_mine, node), (rows_other, node ^ 1)):
            members = [gathered[(which << level) + m] for m in range(1 << level)]
            if level:
                members = [select_lanes(member, 1 << level) for member in members]
                rows = jnp.concatenate([member[:, :lanes] for member in members], 1)
            else:
                rows = members[0]
            scaled = lax.broadcasted_iota(jnp.int32, rows.shape, 0) == 2
            target_ref[rep_levels + level] = jnp.where(
                scaled, rows * ((span // S) << (LEAF_LEVELS + level)), rows
            )

    def leaf_lanes(t):
        return pl.ds(pl.multiple_of(t * span, span), span)

    def wait_piece(win, sem, piece):
        block = win.at[:, leaf_lanes(piece)]
        pltpu.make_async_copy(block, block, sem.at[piece]).wait()

    def near_of(t):
        weight = window_ref[2:3, leaf_lanes(t + 1)]
        self_term = (1.0 - jnp.log(0.5 * weight)) * (0.5 / math.pi)
        total = probe_win[:, leaf_lanes(t + 1)] * (self_term * weight)
        for offset, block, side in ((0, t, 0), (1, leaf_count + 1 + t, 0), (2, t + 1, 1)):
            scale = window_ref[2:3, leaf_lanes(t + offset)] * LOG_SCALE
            a_high, a_low = split_bf16(probe_win[:, leaf_lanes(t + offset)] * scale)
            b_high, b_low = high_ref[block], low_ref[block]
            for a, b in ((a_high, b_high), (a_high, b_low), (a_low, b_high)):
                total = total + lax.dot_general(
                    a, b, (((1,), (side,)), ((), ())), preferred_element_type=jnp.float32
                )
        return total

    def half(index, carry):
        first = index * batch
        products = []

        @pl.when(index == 0)
        def _():
            wait_piece(probe_win, probe_sem, 0)
            wait_piece(probe_win, probe_sem, 1)

        nears = []
        for i in range(batch):
            wait_piece(probe_win, probe_sem, first + i + 2)
        for i in range(batch):
            nears.append(near_of(first + i))
        for i in range(batch):
            t = first + i
            wait_piece(sketch_win, sketch_sem, t)
        for i in range(batch):
            t = first + i
            y = sketch_win[:, leaf_lanes(t)]
            z = y - nears[i]
            z_ref[:, leaf_lanes(t)] = z
            w = probe_win[:, leaf_lanes(t + 1)]
            products.append([matmul(part, z, (1, 1)) for part in (z, y, w)])
        inverse_factor([p[0] for p in products], work_ref)
        hats = []
        for i, p in enumerate(products):
            leaf_inverse[first + i] = work_ref[i]
            hats.append((matmul(p[1], work_ref[i], (1, 1)), matmul(p[2], work_ref[i], (1, 1))))
        if batch == 2:
            (y_a, w_a), (y_b, w_b) = hats
            node = rank * leaf_count + first
            rows_a, rows_b = skeleton(0, node), skeleton(0, node + 1)
            z_a, z_b = off_diagonal(y_a, y_b, w_a, w_b, rows_a, rows_b)
            gram, y_z, w_z = pair_products(z_a, z_b, y_a, y_b, w_a, w_b)
            inverse_factor([gram], work_ref)
            hats = [(matmul(y_z, work_ref[0], (1, 1)), matmul(w_z, work_ref[0], (1, 1)))]
        hats_ref[index, 0] = hats[0][0]
        hats_ref[index, 1] = hats[0][1]
        return carry

    lax.fori_loop(0, leaf_count // batch, half, 0)
    hats = [(hats_ref[i, 0], hats_ref[i, 1]) for i in range(leaf_count // batch)]
    level = batch.bit_length() - 1
    while len(hats) > 1:
        products = []
        for a in range(0, len(hats), 2):
            node = rank * len(hats) + a
            (y_a, w_a), (y_b, w_b) = hats[a], hats[a + 1]
            z_a, z_b = off_diagonal(
                y_a, y_b, w_a, w_b, skeleton(level, node), skeleton(level, node + 1)
            )
            products.append(pair_products(z_a, z_b, y_a, y_b, w_a, w_b))
        inverse_factor([p[0] for p in products], work_ref)
        hats = [
            (matmul(p[1], work_ref[t], (1, 1)), matmul(p[2], work_ref[t], (1, 1)))
            for t, p in enumerate(products)
        ]
        level += 1
    mine_ref[0, 0] = hats[0][0]
    mine_ref[0, 1] = hats[0][1]

    def basis_copy(k):
        rep = rank ^ k
        src = basis_ref.at[pl.ds(pl.multiple_of(rep * columns, 8), columns), :]
        dst = basis_out.at[:, pl.ds(pl.multiple_of(rank * chunk, span), chunk)]
        if k == 0:
            return pltpu.make_async_copy(src, dst, basis_sem.at[0])
        return remote(src, dst, basis_out_sem.at[k], basis_sem.at[k], position, rep)

    def exchange(level, stride):
        copies = []
        peer = peer_of(stride)
        for part in (1, 0):
            copy = remote(
                mine_ref.at[level, part],
                other_ref.at[level, part],
                send_sem.at[level, part],
                recv_sem.at[level, part],
                *peer,
            )
            copy.start()
            copies.append(copy)

        @pl.when(level == 0)
        def _():
            for t in range(leaf_count):
                at = slice(t * span, (t + 1) * span)
                basis_ref[:, at] = matmul(leaf_inverse[t], z_ref[:, at]) * math.sqrt(span)

        @pl.when(level == rep_levels)
        def _():
            for k in range(1, ranks):
                basis_copy(k).start()
            basis_copy(0).start()

        rows_m, rows_o = rows_mine[level], rows_other[level]
        potential = log_kernel(rows_o.T, rows_m)
        y_m, w_m = mine_ref[level, 0], mine_ref[level, 1]
        z_o = -matmul(w_m * rows_m[2:3, :], potential, (1, 1))
        copies[0].wait()
        w_o = other_ref[level, 1]
        z_m = y_m - matmul(w_o * rows_o[2:3, :], potential)
        copies[1].wait()
        y_o = other_ref[level, 0]
        return z_m, z_o + y_o, y_m, y_o, w_m, w_o

    def step(level, stride):
        gram, y_z, w_z = pair_products(*exchange(level, stride))
        inverse_factor([gram], work_ref)
        mine_ref[level + 1, 0] = matmul(y_z, work_ref[0], (1, 1))
        mine_ref[level + 1, 1] = matmul(w_z, work_ref[0], (1, 1))
        return stride * 2

    stride = lax.fori_loop(0, merges - 1, step, 1)
    z_m, z_o = exchange(merges - 1, stride)[:2]
    gram = matmul(z_m, z_m, (1, 1)) + matmul(z_o, z_o, (1, 1))
    inverse_factor([gram], work_ref)
    factor = work_ref[0, own_rows, :] * math.sqrt(2 * S)
    second = lax.rem(position // (1 << (CROSS - 1)), 2) == 1
    top_out[:, :S] = matmul(factor, jnp.where(second, z_o, z_m))
    top_out[:, S:] = matmul(factor, jnp.where(second, z_m, z_o))

    for k in range(ranks):
        basis_copy(k).wait()
    all_sent = probe_ref.at[:, pl.ds(0, (2 * leaf_count + 2) * span)]
    for k in range(1, ranks):
        pltpu.make_async_copy(all_sent, all_sent, out_sem.at[k]).wait()

    @pl.when(rank == 0)
    def _():
        probe_copy(0, 0, False).wait_send()

    @pl.when(rank == ranks - 1)
    def _():
        probe_copy(0, leaf_count + 1, False).wait_send()


def body(curve_coordinates, weighted_density, random_test_matrix, sketch_matrix):
    span = NODES_PER_CELL
    columns, width = random_test_matrix.shape
    ranks = lax.axis_size("rep")
    leaf_count = width // span // ranks
    chunk = leaf_count * span
    merges = LEAF_LEVELS + CROSS - (leaf_count.bit_length() - 1)
    batch = min(2, leaf_count)
    family = 1 << CROSS
    vmem = pl.BlockSpec(memory_space=pltpu.VMEM)
    hbm = pl.BlockSpec(memory_space=pl.ANY)
    f32, bf16 = jnp.float32, jnp.bfloat16
    dma = pltpu.SemaphoreType.DMA
    basis, top = pl.pallas_call(
        functools.partial(tree_kernel, leaf_count),
        out_shape=(
            jax.ShapeDtypeStruct((columns, width), f32),
            jax.ShapeDtypeStruct((columns, 2 * S), f32),
        ),
        in_specs=[vmem, vmem, hbm, hbm],
        out_specs=(hbm, vmem),
        scratch_shapes=[
            pltpu.VMEM((S, chunk + 2 * span), f32),
            pltpu.VMEM((S, chunk), f32),
            pltpu.VMEM((S, chunk), f32),
            pltpu.VMEM((S, chunk), f32),
            pltpu.VMEM((8, width), f32),
            pltpu.VMEM((8, chunk + 2 * span), f32),
            pltpu.VMEM((chunk + 2 * span, 8), f32),
            pltpu.VMEM((2, 2, span), f32),
            pltpu.VMEM((2, 1, span), f32),
            pltpu.VMEM((2 * leaf_count + 1, span, span), bf16),
            pltpu.VMEM((2 * leaf_count + 1, span, span), bf16),
            pltpu.VMEM((LEAF_LEVELS + 1, 8 * (width // span), S), f32),
            pltpu.VMEM((family, 8, S), f32),
            pltpu.VMEM((merges, 8, S), f32),
            pltpu.VMEM((merges, 8, S), f32),
            pltpu.VMEM((merges, 2, S, S), f32),
            pltpu.VMEM((merges, 2, S, S), f32),
            pltpu.VMEM((leaf_count // batch, 2, S, S), f32),
            pltpu.VMEM((leaf_count, S, S), f32),
            pltpu.VMEM((max(2, leaf_count // 2), S, S), f32),
            dma((leaf_count + 2,)),
            dma((leaf_count,)),
            dma((ranks,)),
            dma((2,)),
            dma((4,)),
            dma((4,)),
            dma((2,)),
            dma((merges, 2)),
            dma((merges, 2)),
            dma((ranks,)),
            dma((ranks,)),
        ],
        compiler_params=pltpu.CompilerParams(
            collective_id=0, has_side_effects=True, vmem_limit_bytes=VMEM_LIMIT
        ),
        name="tree",
    )(curve_coordinates, weighted_density[None, :], random_test_matrix, sketch_matrix)
    return (basis, top[None])


def solution(mesh):
    return jax.shard_map(
        body,
        mesh=mesh,
        in_specs=(P(None, "leaf"), P("leaf"), P("rep", "leaf"), P("rep", "leaf")),
        out_specs=(P("rep", "leaf"), P("leaf", "rep", None)),
        check_vma=False,
    )
```

```python
import functools
import math

import jax
import jax.numpy as jnp
from jax import lax
from jax.experimental import pallas as pl
from jax.experimental.pallas import tpu as pltpu
from jax.sharding import PartitionSpec as P

NODES_PER_CELL = 512
S = 128
LEAF_LEVELS = 4
CROSS = 3
NEAR_TILES = (4, 2)
HIGHEST = lax.Precision.HIGHEST
LOG_SCALE = -0.25 / math.pi
VMEM_LIMIT = 60000 * 1024


def matmul(a, b, contract=(1, 0)):
    return lax.dot_general(
        a,
        b,
        (((contract[0],), (contract[1],)), ((), ())),
        precision=HIGHEST,
        preferred_element_type=jnp.float32,
    )


def split_bf16(value):
    high = value.astype(jnp.bfloat16)
    return high, (value - high.astype(jnp.float32)).astype(jnp.bfloat16)


def matmul_split(a, b, contract=(1, 0)):
    a_high, a_low = split_bf16(a)
    b_high, b_low = split_bf16(b)

    def dot(x, y):
        return lax.dot_general(
            x,
            y,
            (((contract[0],), (contract[1],)), ((), ())),
            preferred_element_type=jnp.float32,
        )

    return dot(a_high, b_high) + (dot(a_high, b_low) + dot(a_low, b_high))


def lane_cast(value, k):
    return jnp.take_along_axis(value, jnp.full(value.shape, k, jnp.int32), axis=1)


def row_cast(value, j):
    return jnp.broadcast_to(value[j : j + 1, :], (8, value.shape[1]))


def eliminate(own, k, lane, sub):
    at = [sub == j for j in range(8)]
    in_group = (lane >= k) & (lane < k + 8)
    col = [lane_cast(own, k + l) for l in range(8)]
    rows = jnp.where(in_group, jnp.where(lane == sub + k, 1.0, 0.0), own)
    out = rows
    pivots = rows
    for j in range(0, 8, 2):
        both = at[j] | at[j + 1]
        a, b = row_cast(col[j], j), row_cast(col[j], j + 1)
        c = row_cast(col[j + 1], j + 1)
        det = a * c - b * b
        r, inverse_a = 1.0 / det, 1.0 / a
        first, second = row_cast(rows, j), row_cast(rows, j + 1)
        scale_0 = jnp.where(at[j + 1], -b, col[j + 1] * b - col[j] * c)
        scale_0 = jnp.where(at[j], c, scale_0) * r
        scale_1 = jnp.where(at[j + 1], a, col[j] * b - col[j + 1] * a)
        scale_1 = jnp.where(at[j], -b, scale_1) * r
        out = jnp.where(at[j + 1], second - (b * inverse_a) * first, out)
        out = jnp.where(at[j], first, out)
        pivots = jnp.where(at[j], a, jnp.where(at[j + 1], det * inverse_a, pivots))
        rows = (jnp.where(both, 0.0, rows) + scale_0 * first) + scale_1 * second
        for q in range(j + 2, 8):
            above, below = row_cast(col[q], j), row_cast(col[q], j + 1)
            col[q] = (jnp.where(both, 0.0, col[q]) + scale_0 * above) + scale_1 * below
    root = lax.rsqrt(pivots)
    root = root * (1.5 - 0.5 * pivots * root * root)
    return rows, jnp.where(lane > sub + k, 0.0, out * root)


def inverse_factor(grams, work_ref):
    order = grams[0].shape[0]
    count = order // 8
    near = NEAR_TILES[min(len(grams), 2) - 1]
    lane = lax.broadcasted_iota(jnp.int32, (8, order), 1)
    sub = lax.broadcasted_iota(jnp.int32, (8, order), 0)
    tiles = [[gram[8 * v : 8 * v + 8, :] for v in range(count)] for gram in grams]
    for g in range(count):
        k = 8 * g
        far = g + 1 + near
        in_group = (lane >= k) & (lane < k + 8)
        for i, tile in enumerate(tiles):
            own = tile[g]
            rows, result = eliminate(own, k, lane, sub)
            work_ref[i, k : k + 8, :] = result
            solved = [row_cast(rows, j) for j in range(8)]
            for v in range(g + 1, min(far, count)):
                raw = tile[v]
                total = jnp.where(in_group, 0.0, raw)
                for j in range(8):
                    total = total - lane_cast(raw, k + j) * solved[j]
                tile[v] = total
            if far < count:
                update = matmul(own.T[8 * far :, :], rows)
                for v in range(far, count):
                    kept = jnp.where(in_group, 0.0, tile[v])
                    tile[v] = kept - update[8 * (v - far) : 8 * (v - far) + 8, :]


def peer_of(stride):
    ranks = lax.axis_size("rep")
    place = lax.axis_index("leaf") * ranks + lax.axis_index("rep")
    peer = place + stride * (1 - 2 * ((place // stride) % 2))
    return (peer // ranks, peer % ranks)


def select_lanes(block, stride):
    source = block.shape[1]
    target = source // stride
    take = lax.broadcasted_iota(jnp.int32, (source, target), 0) == stride * lax.broadcasted_iota(
        jnp.int32, (source, target), 1
    )
    return matmul(block, jnp.where(take, 1.0, 0.0))


def log_kernel(source_cols, target_rows):
    delta_x = source_cols[:, 0:1] - target_rows[0:1, :]
    delta_y = source_cols[:, 1:2] - target_rows[1:2, :]
    return jnp.log(delta_x * delta_x + delta_y * delta_y) * LOG_SCALE


def off_diagonal(y_a, y_b, w_a, w_b, rows_a, rows_b):
    potential = log_kernel(rows_b.T, rows_a)
    z_a = y_a - matmul_split(w_b * rows_b[2:3, :], potential)
    z_b = y_b - matmul_split(w_a * rows_a[2:3, :], potential, (1, 1))
    return z_a, z_b


def products_of(z, y, w):
    both = matmul_split(jnp.concatenate([z, y, w], 0), z, (1, 1))
    return both[:S], both[S:]


def hats_of(samples, inverse):
    hats = matmul_split(samples, inverse, (1, 1))
    return hats[:S], hats[S:]


def pair_products(z_a, z_b, y_a, y_b, w_a, w_b):
    return products_of(
        *(jnp.concatenate([a, b], 1) for a, b in ((z_a, z_b), (y_a, y_b), (w_a, w_b)))
    )


def tree_kernel(
    leaf_count,
    coords_ref,
    density_ref,
    probe_ref,
    sketch_ref,
    basis_out,
    top_out,
    probe_win,
    sketch_win,
    z_ref,
    basis_ref,
    points_ref,
    window_ref,
    window_cols,
    halo_xy,
    halo_w,
    high_ref,
    low_ref,
    level_refs,
    gathered,
    rows_mine,
    rows_other,
    mine_ref,
    other_ref,
    hats_ref,
    leaf_inverse,
    work_ref,
    probe_sem,
    sketch_sem,
    out_sem,
    edge_sem,
    point_sem,
    point_out_sem,
    gather_sem,
    send_sem,
    recv_sem,
    basis_sem,
    basis_out_sem,
):
    span = NODES_PER_CELL
    ranks, leaves = lax.axis_size("rep"), lax.axis_size("leaf")
    rank, position = lax.axis_index("rep"), lax.axis_index("leaf")
    columns, width = probe_ref.shape
    total_leaves = width // span
    chunk = leaf_count * span
    local_levels = leaf_count.bit_length() - 1
    rep_levels = LEAF_LEVELS - local_levels
    merges = rep_levels + CROSS
    family = 1 << CROSS
    mesh_id = pl.DeviceIdType.MESH
    after = lax.rem(position + 1, leaves)
    before = lax.rem(position + leaves - 1, leaves)
    barrier = pltpu.get_barrier_semaphore()

    def signal(leaf, rep):
        pl.semaphore_signal(barrier, inc=1, device_id=(leaf, rep), device_id_type=mesh_id)

    @pl.when(rank == 0)
    def _():
        for k in range(ranks):
            signal(before, k)

    @pl.when(rank == ranks - 1)
    def _():
        for k in range(ranks):
            signal(after, k)

    signal(after, rank)
    signal(before, rank)
    for j in range(1, family):
        signal(position ^ j, rank)
    for k in range(1, ranks):
        signal(position, rank ^ k)
    pl.semaphore_wait(barrier, 2 + 2 + (family - 1) + (ranks - 1))

    def remote(src, dst, sent, arrived, leaf, rep):
        return pltpu.make_async_remote_copy(
            src_ref=src,
            dst_ref=dst,
            send_sem=sent,
            recv_sem=arrived,
            device_id=(leaf, rep),
            device_id_type=mesh_id,
        )

    point_copies = []
    for side, leaf, start in ((0, after, width - span), (1, before, 0)):
        for i, (src, dst) in enumerate(((coords_ref, halo_xy), (density_ref, halo_w))):
            point_copies.append(
                remote(
                    src.at[:, pl.ds(start, span)],
                    dst.at[side],
                    point_out_sem.at[2 * side + i],
                    point_sem.at[2 * side + i],
                    leaf,
                    rank,
                )
            )
    for copy in point_copies:
        copy.start()

    own_rows = pl.ds(pl.multiple_of(rank * columns, 8), columns)

    def probe_copy(k, piece, local):
        rep = rank ^ k
        index = rep * leaf_count + piece - 1
        leaf, source = position, index
        if piece == 0:
            leaf = jnp.where(rep == 0, after, position)
            source = jnp.where(rep == 0, total_leaves - 1, index)
        elif piece == leaf_count + 1:
            leaf = jnp.where(rep == ranks - 1, before, position)
            source = jnp.where(rep == ranks - 1, 0, index)
        src = probe_ref.at[:, pl.ds(pl.multiple_of(source * span, span), span)]
        dst = probe_win.at[own_rows, pl.ds(piece * span, span)]
        if local:
            return pltpu.make_async_copy(src, dst, probe_sem.at[piece])
        sent = out_sem.at[k] if k else edge_sem.at[0 if piece == 0 else 1]
        return remote(src, dst, sent, probe_sem.at[piece], leaf, rep)

    def sketch_copy(k, piece):
        rep = rank ^ k
        source = pl.multiple_of((rep * leaf_count + piece) * span, span)
        src = sketch_ref.at[:, pl.ds(source, span)]
        dst = sketch_win.at[own_rows, pl.ds(piece * span, span)]
        if k == 0:
            return pltpu.make_async_copy(src, dst, sketch_sem.at[piece])
        return remote(src, dst, out_sem.at[k], sketch_sem.at[piece], position, rep)

    def start_probe(piece):
        for k in range(1, ranks):
            probe_copy(k, piece, False).start()
        if piece == 0 or piece == leaf_count + 1:
            edge = rank == (0 if piece == 0 else ranks - 1)

            @pl.when(edge)
            def _():
                probe_copy(0, piece, False).start()

            @pl.when(jnp.logical_not(edge))
            def _():
                probe_copy(0, piece, True).start()

        else:
            probe_copy(0, piece, True).start()

    def start_sketch(piece):
        for k in range(1, ranks):
            sketch_copy(k, piece).start()
        sketch_copy(0, piece).start()

    batch = min(2, leaf_count)
    sent_pieces = 0
    for first in range(0, leaf_count, batch):
        while sent_pieces < first + batch + 2:
            start_probe(sent_pieces)
            sent_pieces += 1
        for piece in range(first, first + batch):
            start_sketch(piece)

    points_ref[...] = jnp.zeros_like(points_ref)
    points_ref[0:2, :] = coords_ref[...]
    points_ref[2:3, :] = density_ref[...]
    blocks = [points_ref[:, t * span : (t + 1) * span] for t in range(total_leaves)]
    nodes = select_lanes(jnp.concatenate(blocks, 0), span // S)
    level_refs[0] = nodes
    for level in range(1, LEAF_LEVELS + 1):
        count = total_leaves >> level
        joined = [
            jnp.concatenate([nodes[16 * i : 16 * i + 8], nodes[16 * i + 8 : 16 * i + 16]], 1)
            for i in range(count)
        ]
        nodes = select_lanes(jnp.concatenate(joined, 0), 2)
        level_refs[level, : 8 * count] = nodes
    place = lax.rem(position, family)
    gathered[place] = nodes

    def gather_copy(j):
        return remote(
            gathered.at[place],
            gathered.at[place],
            gather_sem.at[0],
            gather_sem.at[1],
            position ^ j,
            rank,
        )

    for j in range(1, family):
        gather_copy(j).start()

    def skeleton(level, node):
        rows = level_refs[level, pl.ds(pl.multiple_of(node * 8, 8), 8), :]
        scaled = lax.broadcasted_iota(jnp.int32, rows.shape, 0) == 2
        return jnp.where(scaled, rows * ((span // S) << level), rows)

    for level in range(rep_levels):
        node = rank >> level
        rows_mine[level] = skeleton(local_levels + level, node)
        rows_other[level] = skeleton(local_levels + level, node ^ 1)

    for copy in point_copies:
        copy.wait()
    base = rank * chunk
    window_ref[:, span : span + chunk] = points_ref[:, pl.ds(pl.multiple_of(base, span), chunk)]
    for side in range(2):
        at = 0 if side == 0 else span + chunk
        edge = rank == (0 if side == 0 else ranks - 1)
        inner = base - span if side == 0 else base + chunk
        inner = jnp.where(edge, 0, inner)
        own = points_ref[:, pl.ds(pl.multiple_of(inner, span), span)]
        window_ref[:, at : at + span] = own
        window_ref[0:2, at : at + span] = jnp.where(edge, halo_xy[side], own[0:2])
        window_ref[2:3, at : at + span] = jnp.where(edge, halo_w[side], own[2:3])
    for t in range(leaf_count + 2):
        window_cols[t * span : (t + 1) * span, :] = window_ref[:, t * span : (t + 1) * span].T

    def fill(i, carry):
        own = i > leaf_count
        source = jnp.where(own, i - leaf_count, i)
        target = jnp.where(own, i - leaf_count, i + 1)
        cols = window_cols[pl.ds(pl.multiple_of(source * span, span), span), :]
        rows = window_ref[:, pl.ds(pl.multiple_of(target * span, span), span)]
        delta_x = cols[:, 0:1] - rows[0:1, :]
        delta_y = cols[:, 1:2] - rows[1:2, :]
        squared = delta_x * delta_x + delta_y * delta_y
        same = lax.broadcasted_iota(jnp.int32, (span, span), 0) == lax.broadcasted_iota(
            jnp.int32, (span, span), 1
        )
        squared = jnp.where(same & own, 1.0, squared)
        high, low = split_bf16(jnp.log(squared))
        high_ref[i] = high
        low_ref[i] = low
        return carry

    lax.fori_loop(0, 2 * leaf_count + 1, fill, 0)

    for copy_of in range(1):
        seven = gathered.at[pl.ds(0, family - 1)]
        pltpu.make_async_copy(seven, seven, gather_sem.at[1]).wait()
        pltpu.make_async_copy(seven, seven, gather_sem.at[0]).wait()
    for level in range(CROSS):
        lanes = S >> level
        node = place >> level
        for target_ref, which in ((rows_mine, node), (rows_other, node ^ 1)):
            members = [gathered[(which << level) + m] for m in range(1 << level)]
            if level:
                members = [select_lanes(member, 1 << level) for member in members]
                rows = jnp.concatenate([member[:, :lanes] for member in members], 1)
            else:
                rows = members[0]
            scaled = lax.broadcasted_iota(jnp.int32, rows.shape, 0) == 2
            target_ref[rep_levels + level] = jnp.where(
                scaled, rows * ((span // S) << (LEAF_LEVELS + level)), rows
            )

    def leaf_lanes(t):
        return pl.ds(pl.multiple_of(t * span, span), span)

    def wait_piece(win, sem, piece):
        block = win.at[:, leaf_lanes(piece)]
        pltpu.make_async_copy(block, block, sem.at[piece]).wait()

    def near_of(t):
        weight = window_ref[2:3, leaf_lanes(t + 1)]
        self_term = (1.0 - jnp.log(0.5 * weight)) * (0.5 / math.pi)
        total = probe_win[:, leaf_lanes(t + 1)] * (self_term * weight)
        for offset, block, side in ((0, t, 0), (1, leaf_count + 1 + t, 0), (2, t + 1, 1)):
            scale = window_ref[2:3, leaf_lanes(t + offset)] * LOG_SCALE
            a_high, a_low = split_bf16(probe_win[:, leaf_lanes(t + offset)] * scale)
            b_high, b_low = high_ref[block], low_ref[block]
            for a, b in ((a_high, b_high), (a_high, b_low), (a_low, b_high)):
                total = total + lax.dot_general(
                    a, b, (((1,), (side,)), ((), ())), preferred_element_type=jnp.float32
                )
        return total

    def half(index, carry):
        first = index * batch
        products = []

        @pl.when(index == 0)
        def _():
            wait_piece(probe_win, probe_sem, 0)
            wait_piece(probe_win, probe_sem, 1)

        nears = []
        for i in range(batch):
            wait_piece(probe_win, probe_sem, first + i + 2)
        for i in range(batch):
            nears.append(near_of(first + i))
        for i in range(batch):
            t = first + i
            wait_piece(sketch_win, sketch_sem, t)
        for i in range(batch):
            t = first + i
            y = sketch_win[:, leaf_lanes(t)]
            z = y - nears[i]
            z_ref[:, leaf_lanes(t)] = z
            w = probe_win[:, leaf_lanes(t + 1)]
            products.append(products_of(z, y, w))
        inverse_factor([p[0] for p in products], work_ref)
        hats = []
        for i, p in enumerate(products):
            leaf_inverse[first + i] = work_ref[i]
            hats.append(hats_of(p[1], work_ref[i]))
        if batch == 2:
            (y_a, w_a), (y_b, w_b) = hats
            node = rank * leaf_count + first
            rows_a, rows_b = skeleton(0, node), skeleton(0, node + 1)
            z_a, z_b = off_diagonal(y_a, y_b, w_a, w_b, rows_a, rows_b)
            gram, samples = pair_products(z_a, z_b, y_a, y_b, w_a, w_b)
            inverse_factor([gram], work_ref)
            hats = [hats_of(samples, work_ref[0])]
        hats_ref[index, 0] = hats[0][0]
        hats_ref[index, 1] = hats[0][1]
        return carry

    lax.fori_loop(0, leaf_count // batch, half, 0)
    hats = [(hats_ref[i, 0], hats_ref[i, 1]) for i in range(leaf_count // batch)]
    level = batch.bit_length() - 1
    while len(hats) > 1:
        products = []
        for a in range(0, len(hats), 2):
            node = rank * len(hats) + a
            (y_a, w_a), (y_b, w_b) = hats[a], hats[a + 1]
            z_a, z_b = off_diagonal(
                y_a, y_b, w_a, w_b, skeleton(level, node), skeleton(level, node + 1)
            )
            products.append(pair_products(z_a, z_b, y_a, y_b, w_a, w_b))
        inverse_factor([p[0] for p in products], work_ref)
        hats = [hats_of(p[1], work_ref[t]) for t, p in enumerate(products)]
        level += 1
    mine_ref[0, 0] = hats[0][0]
    mine_ref[0, 1] = hats[0][1]

    def basis_copy(k):
        rep = rank ^ k
        src = basis_ref.at[pl.ds(pl.multiple_of(rep * columns, 8), columns), :]
        dst = basis_out.at[:, pl.ds(pl.multiple_of(rank * chunk, span), chunk)]
        if k == 0:
            return pltpu.make_async_copy(src, dst, basis_sem.at[0])
        return remote(src, dst, basis_out_sem.at[k], basis_sem.at[k], position, rep)

    def exchange(level, stride):
        copies = []
        peer = peer_of(stride)
        for part in (1, 0):
            copy = remote(
                mine_ref.at[level, part],
                other_ref.at[level, part],
                send_sem.at[level, part],
                recv_sem.at[level, part],
                *peer,
            )
            copy.start()
            copies.append(copy)

        @pl.when(level == 0)
        def _():
            for t in range(leaf_count):
                at = slice(t * span, (t + 1) * span)
                basis_ref[:, at] = matmul_split(leaf_inverse[t], z_ref[:, at]) * math.sqrt(span)

        @pl.when(level == rep_levels)
        def _():
            for k in range(1, ranks):
                basis_copy(k).start()
            basis_copy(0).start()

        rows_m, rows_o = rows_mine[level], rows_other[level]
        potential = log_kernel(rows_o.T, rows_m)
        y_m, w_m = mine_ref[level, 0], mine_ref[level, 1]
        z_o = -matmul_split(w_m * rows_m[2:3, :], potential, (1, 1))
        copies[0].wait()
        w_o = other_ref[level, 1]
        z_m = y_m - matmul_split(w_o * rows_o[2:3, :], potential)
        copies[1].wait()
        y_o = other_ref[level, 0]
        return z_m, z_o + y_o, y_m, y_o, w_m, w_o

    def step(level, stride):
        gram, samples = pair_products(*exchange(level, stride))
        inverse_factor([gram], work_ref)
        mine_ref[level + 1, 0], mine_ref[level + 1, 1] = hats_of(samples, work_ref[0])
        return stride * 2

    stride = lax.fori_loop(0, merges - 1, step, 1)
    z_m, z_o = exchange(merges - 1, stride)[:2]
    both = jnp.concatenate([z_m, z_o], 1)
    gram = matmul_split(both, both, (1, 1))
    inverse_factor([gram], work_ref)
    factor = work_ref[0, own_rows, :] * math.sqrt(2 * S)
    second = lax.rem(position // (1 << (CROSS - 1)), 2) == 1
    top_out[:, :S] = matmul_split(factor, jnp.where(second, z_o, z_m))
    top_out[:, S:] = matmul_split(factor, jnp.where(second, z_m, z_o))

    for k in range(ranks):
        basis_copy(k).wait()
    all_sent = probe_ref.at[:, pl.ds(0, (2 * leaf_count + 2) * span)]
    for k in range(1, ranks):
        pltpu.make_async_copy(all_sent, all_sent, out_sem.at[k]).wait()

    @pl.when(rank == 0)
    def _():
        probe_copy(0, 0, False).wait_send()

    @pl.when(rank == ranks - 1)
    def _():
        probe_copy(0, leaf_count + 1, False).wait_send()


def body(curve_coordinates, weighted_density, random_test_matrix, sketch_matrix):
    span = NODES_PER_CELL
    columns, width = random_test_matrix.shape
    ranks = lax.axis_size("rep")
    leaf_count = width // span // ranks
    chunk = leaf_count * span
    merges = LEAF_LEVELS + CROSS - (leaf_count.bit_length() - 1)
    batch = min(2, leaf_count)
    family = 1 << CROSS
    vmem = pl.BlockSpec(memory_space=pltpu.VMEM)
    hbm = pl.BlockSpec(memory_space=pl.ANY)
    f32, bf16 = jnp.float32, jnp.bfloat16
    dma = pltpu.SemaphoreType.DMA
    basis, top = pl.pallas_call(
        functools.partial(tree_kernel, leaf_count),
        out_shape=(
            jax.ShapeDtypeStruct((columns, width), f32),
            jax.ShapeDtypeStruct((columns, 2 * S), f32),
        ),
        in_specs=[vmem, vmem, hbm, hbm],
        out_specs=(hbm, vmem),
        scratch_shapes=[
            pltpu.VMEM((S, chunk + 2 * span), f32),
            pltpu.VMEM((S, chunk), f32),
            pltpu.VMEM((S, chunk), f32),
            pltpu.VMEM((S, chunk), f32),
            pltpu.VMEM((8, width), f32),
            pltpu.VMEM((8, chunk + 2 * span), f32),
            pltpu.VMEM((chunk + 2 * span, 8), f32),
            pltpu.VMEM((2, 2, span), f32),
            pltpu.VMEM((2, 1, span), f32),
            pltpu.VMEM((2 * leaf_count + 1, span, span), bf16),
            pltpu.VMEM((2 * leaf_count + 1, span, span), bf16),
            pltpu.VMEM((LEAF_LEVELS + 1, 8 * (width // span), S), f32),
            pltpu.VMEM((family, 8, S), f32),
            pltpu.VMEM((merges, 8, S), f32),
            pltpu.VMEM((merges, 8, S), f32),
            pltpu.VMEM((merges, 2, S, S), f32),
            pltpu.VMEM((merges, 2, S, S), f32),
            pltpu.VMEM((leaf_count // batch, 2, S, S), f32),
            pltpu.VMEM((leaf_count, S, S), f32),
            pltpu.VMEM((max(2, leaf_count // 2), S, S), f32),
            dma((leaf_count + 2,)),
            dma((leaf_count,)),
            dma((ranks,)),
            dma((2,)),
            dma((4,)),
            dma((4,)),
            dma((2,)),
            dma((merges, 2)),
            dma((merges, 2)),
            dma((ranks,)),
            dma((ranks,)),
        ],
        compiler_params=pltpu.CompilerParams(
            collective_id=0, has_side_effects=True, vmem_limit_bytes=VMEM_LIMIT
        ),
        name="tree",
    )(curve_coordinates, weighted_density[None, :], random_test_matrix, sketch_matrix)
    return (basis, top[None])


def solution(mesh):
    return jax.shard_map(
        body,
        mesh=mesh,
        in_specs=(P(None, "leaf"), P("leaf"), P("rep", "leaf"), P("rep", "leaf")),
        out_specs=(P("rep", "leaf"), P("leaf", "rep", None)),
        check_vma=False,
    )
```

```python
import functools
import math

import jax
import jax.numpy as jnp
from jax import lax
from jax.experimental import pallas as pl
from jax.experimental.pallas import tpu as pltpu
from jax.sharding import PartitionSpec as P

NODES_PER_CELL = 512
S = 128
LEAF_LEVELS = 4
CROSS = 3
NEAR_TILES = (4, 2)
SEND_AFTER = 2
HIGHEST = lax.Precision.HIGHEST
LOG_SCALE = -0.25 / math.pi
VMEM_LIMIT = 60000 * 1024


def matmul(a, b, contract=(1, 0)):
    return lax.dot_general(
        a,
        b,
        (((contract[0],), (contract[1],)), ((), ())),
        precision=HIGHEST,
        preferred_element_type=jnp.float32,
    )


def split_bf16(value):
    high = value.astype(jnp.bfloat16)
    return high, (value - high.astype(jnp.float32)).astype(jnp.bfloat16)


def matmul_split(a, b, contract=(1, 0)):
    a_high, a_low = split_bf16(a)
    b_high, b_low = split_bf16(b)

    def dot(x, y):
        return lax.dot_general(
            x,
            y,
            (((contract[0],), (contract[1],)), ((), ())),
            preferred_element_type=jnp.float32,
        )

    return dot(a_high, b_high) + (dot(a_high, b_low) + dot(a_low, b_high))


def lane_cast(value, k):
    return jnp.take_along_axis(value, jnp.full(value.shape, k, jnp.int32), axis=1)


def row_cast(value, j):
    return jnp.broadcast_to(value[j : j + 1, :], (8, value.shape[1]))


def eliminate(own, k, lane, sub):
    at = [sub == j for j in range(8)]
    in_group = (lane >= k) & (lane < k + 8)
    col = [lane_cast(own, k + l) for l in range(8)]
    rows = jnp.where(in_group, jnp.where(lane == sub + k, 1.0, 0.0), own)
    out = rows
    pivots = rows
    for j in range(0, 8, 2):
        both = at[j] | at[j + 1]
        a, b = row_cast(col[j], j), row_cast(col[j], j + 1)
        c = row_cast(col[j + 1], j + 1)
        det = a * c - b * b
        r, inverse_a = 1.0 / det, 1.0 / a
        first, second = row_cast(rows, j), row_cast(rows, j + 1)
        scale_0 = jnp.where(at[j + 1], -b, col[j + 1] * b - col[j] * c)
        scale_0 = jnp.where(at[j], c, scale_0) * r
        scale_1 = jnp.where(at[j + 1], a, col[j] * b - col[j + 1] * a)
        scale_1 = jnp.where(at[j], -b, scale_1) * r
        out = jnp.where(at[j + 1], second - (b * inverse_a) * first, out)
        out = jnp.where(at[j], first, out)
        pivots = jnp.where(at[j], a, jnp.where(at[j + 1], det * inverse_a, pivots))
        rows = (jnp.where(both, 0.0, rows) + scale_0 * first) + scale_1 * second
        for q in range(j + 2, 8):
            above, below = row_cast(col[q], j), row_cast(col[q], j + 1)
            col[q] = (jnp.where(both, 0.0, col[q]) + scale_0 * above) + scale_1 * below
    root = lax.rsqrt(pivots)
    root = root * (1.5 - 0.5 * pivots * root * root)
    return rows, jnp.where(lane > sub + k, 0.0, out * root)


def inverse_factor(grams, work_ref, hooks={}):
    order = grams[0].shape[0]
    count = order // 8
    near = NEAR_TILES[min(len(grams), 2) - 1]
    lane = lax.broadcasted_iota(jnp.int32, (8, order), 1)
    sub = lax.broadcasted_iota(jnp.int32, (8, order), 0)
    tiles = [[gram[8 * v : 8 * v + 8, :] for v in range(count)] for gram in grams]
    for g in range(count):
        k = 8 * g
        far = g + 1 + near
        in_group = (lane >= k) & (lane < k + 8)
        for i, tile in enumerate(tiles):
            own = tile[g]
            rows, result = eliminate(own, k, lane, sub)
            work_ref[i, k : k + 8, :] = result
            solved = [row_cast(rows, j) for j in range(8)]
            for v in range(g + 1, min(far, count)):
                raw = tile[v]
                total = jnp.where(in_group, 0.0, raw)
                for j in range(8):
                    total = total - lane_cast(raw, k + j) * solved[j]
                tile[v] = total
            if far < count:
                update = matmul(own.T[8 * far :, :], rows)
                for v in range(far, count):
                    kept = jnp.where(in_group, 0.0, tile[v])
                    tile[v] = kept - update[8 * (v - far) : 8 * (v - far) + 8, :]
        if g in hooks:
            hooks[g]()


def peer_of(stride):
    ranks = lax.axis_size("rep")
    place = lax.axis_index("leaf") * ranks + lax.axis_index("rep")
    peer = place + stride * (1 - 2 * ((place // stride) % 2))
    return (peer // ranks, peer % ranks)


def select_lanes(block, stride):
    source = block.shape[1]
    target = source // stride
    take = lax.broadcasted_iota(jnp.int32, (source, target), 0) == stride * lax.broadcasted_iota(
        jnp.int32, (source, target), 1
    )
    return matmul(block, jnp.where(take, 1.0, 0.0))


def log_kernel(source_cols, target_rows):
    delta_x = source_cols[:, 0:1] - target_rows[0:1, :]
    delta_y = source_cols[:, 1:2] - target_rows[1:2, :]
    return jnp.log(delta_x * delta_x + delta_y * delta_y) * LOG_SCALE


def off_diagonal(y_a, y_b, w_a, w_b, rows_a, rows_b):
    potential = log_kernel(rows_b.T, rows_a)
    z_a = y_a - matmul_split(w_b * rows_b[2:3, :], potential)
    z_b = y_b - matmul_split(w_a * rows_a[2:3, :], potential, (1, 1))
    return z_a, z_b


def products_of(z, y, w):
    gram = matmul_split(z, z, (1, 1))
    return gram, matmul_split(jnp.concatenate([y, w], 0), z, (1, 1))


def hats_of(samples, inverse):
    hats = matmul_split(samples, inverse, (1, 1))
    return hats[:S], hats[S:]


def swap_halves(value):
    return pltpu.roll(value, S // 2, 1)


def merge_halves(left, right):
    lane = lax.broadcasted_iota(jnp.int32, left.shape, 1)
    return jnp.where(lane < S // 2, left, right)


def half_hats(samples, rows):
    zero = jnp.zeros_like(rows)
    spread = jnp.concatenate(
        [jnp.concatenate([rows, zero], 1), jnp.concatenate([zero, rows], 1)], 0
    )
    return matmul_split(samples, spread, (1, 1))


def pair_products(z_a, z_b, y_a, y_b, w_a, w_b):
    return products_of(
        *(jnp.concatenate([a, b], 1) for a, b in ((z_a, z_b), (y_a, y_b), (w_a, w_b)))
    )


def tree_kernel(
    leaf_count,
    coords_ref,
    density_ref,
    probe_ref,
    sketch_ref,
    basis_out,
    top_out,
    probe_win,
    sketch_win,
    z_ref,
    basis_ref,
    points_ref,
    window_ref,
    window_cols,
    halo_xy,
    halo_w,
    high_ref,
    low_ref,
    level_refs,
    gathered,
    rows_mine,
    rows_other,
    mine_ref,
    other_ref,
    hats_ref,
    leaf_inverse,
    work_ref,
    probe_sem,
    sketch_sem,
    out_sem,
    edge_sem,
    point_sem,
    point_out_sem,
    gather_sem,
    send_sem,
    recv_sem,
    basis_sem,
    basis_out_sem,
):
    span = NODES_PER_CELL
    ranks, leaves = lax.axis_size("rep"), lax.axis_size("leaf")
    rank, position = lax.axis_index("rep"), lax.axis_index("leaf")
    columns, width = probe_ref.shape
    total_leaves = width // span
    chunk = leaf_count * span
    local_levels = leaf_count.bit_length() - 1
    rep_levels = LEAF_LEVELS - local_levels
    merges = rep_levels + CROSS
    family = 1 << CROSS
    mesh_id = pl.DeviceIdType.MESH
    after = lax.rem(position + 1, leaves)
    before = lax.rem(position + leaves - 1, leaves)
    barrier = pltpu.get_barrier_semaphore()

    def signal(leaf, rep):
        pl.semaphore_signal(barrier, inc=1, device_id=(leaf, rep), device_id_type=mesh_id)

    @pl.when(rank == 0)
    def _():
        for k in range(ranks):
            signal(before, k)

    @pl.when(rank == ranks - 1)
    def _():
        for k in range(ranks):
            signal(after, k)

    signal(after, rank)
    signal(before, rank)
    for j in range(1, family):
        signal(position ^ j, rank)
    for k in range(1, ranks):
        signal(position, rank ^ k)
    pl.semaphore_wait(barrier, 2 + 2 + (family - 1) + (ranks - 1))

    def remote(src, dst, sent, arrived, leaf, rep):
        return pltpu.make_async_remote_copy(
            src_ref=src,
            dst_ref=dst,
            send_sem=sent,
            recv_sem=arrived,
            device_id=(leaf, rep),
            device_id_type=mesh_id,
        )

    point_copies = []
    for side, leaf, start in ((0, after, width - span), (1, before, 0)):
        for i, (src, dst) in enumerate(((coords_ref, halo_xy), (density_ref, halo_w))):
            point_copies.append(
                remote(
                    src.at[:, pl.ds(start, span)],
                    dst.at[side],
                    point_out_sem.at[2 * side + i],
                    point_sem.at[2 * side + i],
                    leaf,
                    rank,
                )
            )
    for copy in point_copies:
        copy.start()

    own_rows = pl.ds(pl.multiple_of(rank * columns, 8), columns)

    def probe_copy(k, piece, local):
        rep = rank ^ k
        index = rep * leaf_count + piece - 1
        leaf, source = position, index
        if piece == 0:
            leaf = jnp.where(rep == 0, after, position)
            source = jnp.where(rep == 0, total_leaves - 1, index)
        elif piece == leaf_count + 1:
            leaf = jnp.where(rep == ranks - 1, before, position)
            source = jnp.where(rep == ranks - 1, 0, index)
        src = probe_ref.at[:, pl.ds(pl.multiple_of(source * span, span), span)]
        dst = probe_win.at[own_rows, pl.ds(piece * span, span)]
        if local:
            return pltpu.make_async_copy(src, dst, probe_sem.at[piece])
        sent = out_sem.at[k] if k else edge_sem.at[0 if piece == 0 else 1]
        return remote(src, dst, sent, probe_sem.at[piece], leaf, rep)

    def sketch_copy(k, piece):
        rep = rank ^ k
        source = pl.multiple_of((rep * leaf_count + piece) * span, span)
        src = sketch_ref.at[:, pl.ds(source, span)]
        dst = sketch_win.at[own_rows, pl.ds(piece * span, span)]
        if k == 0:
            return pltpu.make_async_copy(src, dst, sketch_sem.at[piece])
        return remote(src, dst, out_sem.at[k], sketch_sem.at[piece], position, rep)

    def start_probe(piece):
        for k in range(1, ranks):
            probe_copy(k, piece, False).start()
        if piece == 0 or piece == leaf_count + 1:
            edge = rank == (0 if piece == 0 else ranks - 1)

            @pl.when(edge)
            def _():
                probe_copy(0, piece, False).start()

            @pl.when(jnp.logical_not(edge))
            def _():
                probe_copy(0, piece, True).start()

        else:
            probe_copy(0, piece, True).start()

    def start_sketch(piece):
        for k in range(1, ranks):
            sketch_copy(k, piece).start()
        sketch_copy(0, piece).start()

    batch = min(2, leaf_count)
    sent_pieces = 0
    for first in range(0, leaf_count, batch):
        while sent_pieces < first + batch + 2:
            start_probe(sent_pieces)
            sent_pieces += 1
        for piece in range(first, first + batch):
            start_sketch(piece)

    points_ref[...] = jnp.zeros_like(points_ref)
    points_ref[0:2, :] = coords_ref[...]
    points_ref[2:3, :] = density_ref[...]
    blocks = [points_ref[:, t * span : (t + 1) * span] for t in range(total_leaves)]
    nodes = select_lanes(jnp.concatenate(blocks, 0), span // S)
    level_refs[0] = nodes
    for level in range(1, LEAF_LEVELS + 1):
        count = total_leaves >> level
        joined = [
            jnp.concatenate([nodes[16 * i : 16 * i + 8], nodes[16 * i + 8 : 16 * i + 16]], 1)
            for i in range(count)
        ]
        nodes = select_lanes(jnp.concatenate(joined, 0), 2)
        level_refs[level, : 8 * count] = nodes
    place = lax.rem(position, family)
    gathered[place] = nodes

    def gather_copy(j):
        return remote(
            gathered.at[place],
            gathered.at[place],
            gather_sem.at[0],
            gather_sem.at[1],
            position ^ j,
            rank,
        )

    for j in range(1, family):
        gather_copy(j).start()

    def skeleton(level, node):
        rows = level_refs[level, pl.ds(pl.multiple_of(node * 8, 8), 8), :]
        scaled = lax.broadcasted_iota(jnp.int32, rows.shape, 0) == 2
        return jnp.where(scaled, rows * ((span // S) << level), rows)

    for level in range(rep_levels):
        node = rank >> level
        rows_mine[level] = skeleton(local_levels + level, node)
        rows_other[level] = skeleton(local_levels + level, node ^ 1)

    for copy in point_copies:
        copy.wait()
    base = rank * chunk
    window_ref[:, span : span + chunk] = points_ref[:, pl.ds(pl.multiple_of(base, span), chunk)]
    for side in range(2):
        at = 0 if side == 0 else span + chunk
        edge = rank == (0 if side == 0 else ranks - 1)
        inner = base - span if side == 0 else base + chunk
        inner = jnp.where(edge, 0, inner)
        own = points_ref[:, pl.ds(pl.multiple_of(inner, span), span)]
        window_ref[:, at : at + span] = own
        window_ref[0:2, at : at + span] = jnp.where(edge, halo_xy[side], own[0:2])
        window_ref[2:3, at : at + span] = jnp.where(edge, halo_w[side], own[2:3])
    for t in range(leaf_count + 2):
        window_cols[t * span : (t + 1) * span, :] = window_ref[:, t * span : (t + 1) * span].T

    def fill(i, carry):
        own = i > leaf_count
        source = jnp.where(own, i - leaf_count, i)
        target = jnp.where(own, i - leaf_count, i + 1)
        cols = window_cols[pl.ds(pl.multiple_of(source * span, span), span), :]
        rows = window_ref[:, pl.ds(pl.multiple_of(target * span, span), span)]
        delta_x = cols[:, 0:1] - rows[0:1, :]
        delta_y = cols[:, 1:2] - rows[1:2, :]
        squared = delta_x * delta_x + delta_y * delta_y
        same = lax.broadcasted_iota(jnp.int32, (span, span), 0) == lax.broadcasted_iota(
            jnp.int32, (span, span), 1
        )
        squared = jnp.where(same & own, 1.0, squared)
        high, low = split_bf16(jnp.log(squared))
        high_ref[i] = high
        low_ref[i] = low
        return carry

    lax.fori_loop(0, 2 * leaf_count + 1, fill, 0)

    for copy_of in range(1):
        seven = gathered.at[pl.ds(0, family - 1)]
        pltpu.make_async_copy(seven, seven, gather_sem.at[1]).wait()
        pltpu.make_async_copy(seven, seven, gather_sem.at[0]).wait()
    for level in range(CROSS):
        lanes = S >> level
        node = place >> level
        for target_ref, which in ((rows_mine, node), (rows_other, node ^ 1)):
            members = [gathered[(which << level) + m] for m in range(1 << level)]
            if level:
                members = [select_lanes(member, 1 << level) for member in members]
                rows = jnp.concatenate([member[:, :lanes] for member in members], 1)
            else:
                rows = members[0]
            scaled = lax.broadcasted_iota(jnp.int32, rows.shape, 0) == 2
            target_ref[rep_levels + level] = jnp.where(
                scaled, rows * ((span // S) << (LEAF_LEVELS + level)), rows
            )

    def leaf_lanes(t):
        return pl.ds(pl.multiple_of(t * span, span), span)

    def wait_piece(win, sem, piece):
        block = win.at[:, leaf_lanes(piece)]
        pltpu.make_async_copy(block, block, sem.at[piece]).wait()

    def near_of(t):
        weight = window_ref[2:3, leaf_lanes(t + 1)]
        self_term = (1.0 - jnp.log(0.5 * weight)) * (0.5 / math.pi)
        total = probe_win[:, leaf_lanes(t + 1)] * (self_term * weight)
        for offset, block, side in ((0, t, 0), (1, leaf_count + 1 + t, 0), (2, t + 1, 1)):
            scale = window_ref[2:3, leaf_lanes(t + offset)] * LOG_SCALE
            a_high, a_low = split_bf16(probe_win[:, leaf_lanes(t + offset)] * scale)
            b_high, b_low = high_ref[block], low_ref[block]
            for a, b in ((a_high, b_high), (a_high, b_low), (a_low, b_high)):
                total = total + lax.dot_general(
                    a, b, (((1,), (side,)), ((), ())), preferred_element_type=jnp.float32
                )
        return total

    def half(index, carry):
        first = index * batch
        products = []

        @pl.when(index == 0)
        def _():
            wait_piece(probe_win, probe_sem, 0)
            wait_piece(probe_win, probe_sem, 1)

        nears = []
        for i in range(batch):
            wait_piece(probe_win, probe_sem, first + i + 2)
        for i in range(batch):
            nears.append(near_of(first + i))
        for i in range(batch):
            t = first + i
            wait_piece(sketch_win, sketch_sem, t)
            y = sketch_win[:, leaf_lanes(t)]
            z = y - nears[i]
            z_ref[:, leaf_lanes(t)] = z
            w = probe_win[:, leaf_lanes(t + 1)]
            products.append(products_of(z, y, w))
        inverse_factor([p[0] for p in products], work_ref)
        for i, p in enumerate(products):
            leaf_inverse[first + i] = work_ref[i]
            hats_ref[first + i, 0], hats_ref[first + i, 1] = hats_of(p[1], work_ref[i])
        return carry

    def exchange_copy(level, part, stride):
        return remote(
            mine_ref.at[level, part],
            other_ref.at[level, part],
            send_sem.at[level, part],
            recv_sem.at[level, part],
            *peer_of(stride),
        )

    def finish(gram, samples, level, stride):
        stacked = jnp.concatenate([samples[:S], samples[S:]], 1)
        middle = S // 2

        def store(part):
            rows = work_ref[0, part * middle : (part + 1) * middle, :]
            mine_ref[level, part] = half_hats(stacked, rows)

        hooks = {
            middle // 8 - 1: lambda: store(0),
            middle // 8 + SEND_AFTER: lambda: exchange_copy(level, 0, stride).start(),
        }
        inverse_factor([gram], work_ref, hooks)
        store(1)
        exchange_copy(level, 1, stride).start()

    lax.fori_loop(0, leaf_count // batch, half, 0)
    hats = [(hats_ref[i, 0], hats_ref[i, 1]) for i in range(leaf_count)]
    for level in range(local_levels):
        products = []
        for a in range(0, len(hats), 2):
            node = rank * len(hats) + a
            (y_a, w_a), (y_b, w_b) = hats[a], hats[a + 1]
            z_a, z_b = off_diagonal(
                y_a, y_b, w_a, w_b, skeleton(level, node), skeleton(level, node + 1)
            )
            products.append(pair_products(z_a, z_b, y_a, y_b, w_a, w_b))
        if len(products) == 1:
            finish(*products[0], 0, 1)
        else:
            inverse_factor([p[0] for p in products], work_ref)
            hats = [hats_of(p[1], work_ref[t]) for t, p in enumerate(products)]
    if local_levels == 0:
        y, w = hats[0]
        mine_ref[0, 0] = merge_halves(y, swap_halves(w))
        mine_ref[0, 1] = merge_halves(swap_halves(y), w)
        exchange_copy(0, 0, 1).start()
        exchange_copy(0, 1, 1).start()

    def basis_copy(k):
        rep = rank ^ k
        src = basis_ref.at[pl.ds(pl.multiple_of(rep * columns, 8), columns), :]
        dst = basis_out.at[:, pl.ds(pl.multiple_of(rank * chunk, span), chunk)]
        if k == 0:
            return pltpu.make_async_copy(src, dst, basis_sem.at[0])
        return remote(src, dst, basis_out_sem.at[k], basis_sem.at[k], position, rep)

    def exchange(level, stride):
        @pl.when(level == 0)
        def _():
            for t in range(leaf_count):
                at = slice(t * span, (t + 1) * span)
                basis_ref[:, at] = matmul_split(leaf_inverse[t], z_ref[:, at]) * math.sqrt(span)

        @pl.when(level == rep_levels)
        def _():
            for k in range(1, ranks):
                basis_copy(k).start()
            basis_copy(0).start()

        rows_m, rows_o = rows_mine[level], rows_other[level]
        cols_o = rows_o.T
        potential = log_kernel(cols_o, rows_m)
        scaled = potential * cols_o[:, 2:3]
        middle = S // 2
        zero = jnp.zeros((middle, S), jnp.float32)
        top, low = mine_ref[level, 0], mine_ref[level, 1]
        y_m, w_m = merge_halves(top, swap_halves(low)), merge_halves(swap_halves(top), low)
        near_o = matmul_split(w_m * rows_m[2:3, :], potential, (1, 1))
        exchange_copy(level, 0, stride).wait()
        top = other_ref[level, 0]
        z_m = y_m - matmul_split(top, jnp.concatenate([zero, scaled[:middle]], 0))
        exchange_copy(level, 1, stride).wait()
        low = other_ref[level, 1]
        z_m = z_m - matmul_split(low, jnp.concatenate([zero, scaled[middle:]], 0))
        y_o, w_o = merge_halves(top, swap_halves(low)), merge_halves(swap_halves(top), low)
        return z_m, y_o - near_o, y_m, y_o, w_m, w_o

    def step(level, stride):
        gram, samples = pair_products(*exchange(level, stride))
        finish(gram, samples, level + 1, stride * 2)
        return stride * 2

    stride = lax.fori_loop(0, merges - 1, step, 1)
    z_m, z_o = exchange(merges - 1, stride)[:2]
    both = jnp.concatenate([z_m, z_o], 1)
    gram = matmul_split(both, both, (1, 1))
    inverse_factor([gram], work_ref)
    factor = work_ref[0, own_rows, :] * math.sqrt(2 * S)
    second = lax.rem(position // (1 << (CROSS - 1)), 2) == 1
    top_out[:, :S] = matmul_split(factor, jnp.where(second, z_o, z_m))
    top_out[:, S:] = matmul_split(factor, jnp.where(second, z_m, z_o))

    for k in range(ranks):
        basis_copy(k).wait()
    all_sent = probe_ref.at[:, pl.ds(0, (2 * leaf_count + 2) * span)]
    for k in range(1, ranks):
        pltpu.make_async_copy(all_sent, all_sent, out_sem.at[k]).wait()

    @pl.when(rank == 0)
    def _():
        probe_copy(0, 0, False).wait_send()

    @pl.when(rank == ranks - 1)
    def _():
        probe_copy(0, leaf_count + 1, False).wait_send()


def body(curve_coordinates, weighted_density, random_test_matrix, sketch_matrix):
    span = NODES_PER_CELL
    columns, width = random_test_matrix.shape
    ranks = lax.axis_size("rep")
    leaf_count = width // span // ranks
    chunk = leaf_count * span
    merges = LEAF_LEVELS + CROSS - (leaf_count.bit_length() - 1)
    family = 1 << CROSS
    vmem = pl.BlockSpec(memory_space=pltpu.VMEM)
    hbm = pl.BlockSpec(memory_space=pl.ANY)
    f32, bf16 = jnp.float32, jnp.bfloat16
    dma = pltpu.SemaphoreType.DMA
    basis, top = pl.pallas_call(
        functools.partial(tree_kernel, leaf_count),
        out_shape=(
            pltpu.VMEM((columns, width), f32),
            jax.ShapeDtypeStruct((columns, 2 * S), f32),
        ),
        in_specs=[vmem, vmem, hbm, hbm],
        out_specs=(vmem, vmem),
        scratch_shapes=[
            pltpu.VMEM((S, chunk + 2 * span), f32),
            pltpu.VMEM((S, chunk), f32),
            pltpu.VMEM((S, chunk), f32),
            pltpu.VMEM((S, chunk), f32),
            pltpu.VMEM((8, width), f32),
            pltpu.VMEM((8, chunk + 2 * span), f32),
            pltpu.VMEM((chunk + 2 * span, 8), f32),
            pltpu.VMEM((2, 2, span), f32),
            pltpu.VMEM((2, 1, span), f32),
            pltpu.VMEM((2 * leaf_count + 1, span, span), bf16),
            pltpu.VMEM((2 * leaf_count + 1, span, span), bf16),
            pltpu.VMEM((LEAF_LEVELS + 1, 8 * (width // span), S), f32),
            pltpu.VMEM((family, 8, S), f32),
            pltpu.VMEM((merges, 8, S), f32),
            pltpu.VMEM((merges, 8, S), f32),
            pltpu.VMEM((merges, 2, S, S), f32),
            pltpu.VMEM((merges, 2, S, S), f32),
            pltpu.VMEM((leaf_count, 2, S, S), f32),
            pltpu.VMEM((leaf_count, S, S), f32),
            pltpu.VMEM((max(2, leaf_count // 2), S, S), f32),
            dma((leaf_count + 2,)),
            dma((leaf_count,)),
            dma((ranks,)),
            dma((2,)),
            dma((4,)),
            dma((4,)),
            dma((2,)),
            dma((merges, 2)),
            dma((merges, 2)),
            dma((ranks,)),
            dma((ranks,)),
        ],
        compiler_params=pltpu.CompilerParams(
            collective_id=0, has_side_effects=True, vmem_limit_bytes=VMEM_LIMIT
        ),
        name="tree",
    )(curve_coordinates, weighted_density[None, :], random_test_matrix, sketch_matrix)
    return (basis, top[None])


def solution(mesh):
    return jax.shard_map(
        body,
        mesh=mesh,
        in_specs=(P(None, "leaf"), P("leaf"), P("rep", "leaf"), P("rep", "leaf")),
        out_specs=(P("rep", "leaf"), P("leaf", "rep", None)),
        check_vma=False,
    )
```

```python
import functools
import math

import jax
import jax.numpy as jnp
from jax import lax
from jax.experimental import pallas as pl
from jax.experimental.pallas import tpu as pltpu
from jax.sharding import PartitionSpec as P

NODES_PER_CELL = 512
S = 128
LEAF_LEVELS = 4
CROSS = 3
NEAR_TILES = (3, 2)
SEND_AFTER = 2
HIGHEST = lax.Precision.HIGHEST
LOG_SCALE = -0.25 / math.pi
VMEM_LIMIT = 60000 * 1024


def matmul(a, b, contract=(1, 0)):
    return lax.dot_general(
        a,
        b,
        (((contract[0],), (contract[1],)), ((), ())),
        precision=HIGHEST,
        preferred_element_type=jnp.float32,
    )


def split_bf16(value):
    high = value.astype(jnp.bfloat16)
    return high, (value - high.astype(jnp.float32)).astype(jnp.bfloat16)


def matmul_split(a, b, contract=(1, 0)):
    a_high, a_low = split_bf16(a)
    b_high, b_low = split_bf16(b)

    def dot(x, y):
        return lax.dot_general(
            x,
            y,
            (((contract[0],), (contract[1],)), ((), ())),
            preferred_element_type=jnp.float32,
        )

    return dot(a_high, b_high) + (dot(a_high, b_low) + dot(a_low, b_high))


def lane_cast(value, k):
    return jnp.take_along_axis(value, jnp.full(value.shape, k, jnp.int32), axis=1)


def row_cast(value, j):
    return jnp.broadcast_to(value[j : j + 1, :], (8, value.shape[1]))


def eliminate(own, col, following, k, lane, sub):
    at = [sub == j for j in range(8)]
    in_group = (lane >= k) & (lane < k + 8)
    rows = jnp.where(in_group, jnp.where(lane == sub + k, 1.0, 0.0), own)
    out = rows
    pivots = rows
    if following is not None:
        side = [lane_cast(following, k + l) for l in range(8)]
        ahead = [lane_cast(following, k + 8 + l) for l in range(8)]
        following = jnp.where(in_group, 0.0, following)
    for j in range(0, 8, 2):
        both = at[j] | at[j + 1]
        a, b = row_cast(col[j], j), row_cast(col[j], j + 1)
        c = row_cast(col[j + 1], j + 1)
        det = a * c - b * b
        r, inverse_a = 1.0 / det, 1.0 / a
        first, second = row_cast(rows, j), row_cast(rows, j + 1)
        scale_0 = jnp.where(at[j + 1], -b, col[j + 1] * b - col[j] * c)
        scale_0 = jnp.where(at[j], c, scale_0) * r
        scale_1 = jnp.where(at[j + 1], a, col[j] * b - col[j + 1] * a)
        scale_1 = jnp.where(at[j], -b, scale_1) * r
        out = jnp.where(at[j + 1], second - (b * inverse_a) * first, out)
        out = jnp.where(at[j], first, out)
        pivots = jnp.where(at[j], a, jnp.where(at[j + 1], det * inverse_a, pivots))
        rows = (jnp.where(both, 0.0, rows) + scale_0 * first) + scale_1 * second
        if following is not None:
            side_0 = (side[j] * c - side[j + 1] * b) * r
            side_1 = (side[j + 1] * a - side[j] * b) * r
            following = following - side_0 * first - side_1 * second
            for q in range(8):
                left, right = row_cast(side[j], q), row_cast(side[j + 1], q)
                ahead[q] = ahead[q] - side_0 * left - side_1 * right
        for q in range(j + 2, 8):
            above, below = row_cast(col[q], j), row_cast(col[q], j + 1)
            if following is not None:
                side[q] = side[q] - side_0 * above - side_1 * below
            col[q] = (jnp.where(both, 0.0, col[q]) + scale_0 * above) + scale_1 * below
    root = lax.rsqrt(pivots)
    root = root * (1.5 - 0.5 * pivots * root * root)
    result = jnp.where(lane > sub + k, 0.0, out * root)
    return rows, result, following, ahead if following is not None else None


def inverse_factor(grams, work_ref, hooks={}):
    order = grams[0].shape[0]
    count = order // 8
    alone = len(grams) == 1
    near = NEAR_TILES[0 if alone else 1]
    lane = lax.broadcasted_iota(jnp.int32, (8, order), 1)
    sub = lax.broadcasted_iota(jnp.int32, (8, order), 0)
    tiles = [[gram[8 * v : 8 * v + 8, :] for v in range(count)] for gram in grams]
    columns = [None for _ in grams]
    for g in range(count):
        k = 8 * g
        far = g + 1 + near
        in_group = (lane >= k) & (lane < k + 8)
        for i, tile in enumerate(tiles):
            own = tile[g]
            col = columns[i]
            if col is None:
                col = [lane_cast(own, k + l) for l in range(8)]
            following = tile[g + 1] if alone and g + 1 < count else None
            rows, result, following, columns[i] = eliminate(own, col, following, k, lane, sub)
            work_ref[i, k : k + 8, :] = result
            if following is not None:
                tile[g + 1] = following
            solved = [row_cast(rows, j) for j in range(8)]
            for v in range(g + 2 if alone else g + 1, min(far, count)):
                raw = tile[v]
                terms = [lane_cast(raw, k + j) * solved[j] for j in range(8)]
                while len(terms) > 1:
                    terms = [a + b for a, b in zip(terms[::2], terms[1::2])]
                tile[v] = jnp.where(in_group, 0.0, raw) - terms[0]
            if far < count:
                update = matmul(own.T[8 * far :, :], rows)
                for v in range(far, count):
                    kept = jnp.where(in_group, 0.0, tile[v])
                    tile[v] = kept - update[8 * (v - far) : 8 * (v - far) + 8, :]
        if g in hooks:
            hooks[g]()


def peer_of(stride):
    ranks = lax.axis_size("rep")
    place = lax.axis_index("leaf") * ranks + lax.axis_index("rep")
    peer = place + stride * (1 - 2 * ((place // stride) % 2))
    return (peer // ranks, peer % ranks)


def select_lanes(block, stride):
    source = block.shape[1]
    target = source // stride
    take = lax.broadcasted_iota(jnp.int32, (source, target), 0) == stride * lax.broadcasted_iota(
        jnp.int32, (source, target), 1
    )
    return matmul(block, jnp.where(take, 1.0, 0.0))


def log_kernel(source_cols, target_rows):
    delta_x = source_cols[:, 0:1] - target_rows[0:1, :]
    delta_y = source_cols[:, 1:2] - target_rows[1:2, :]
    return jnp.log(delta_x * delta_x + delta_y * delta_y) * LOG_SCALE


def off_diagonal(y_a, y_b, w_a, w_b, rows_a, rows_b):
    potential = log_kernel(rows_b.T, rows_a)
    z_a = y_a - matmul_split(w_b * rows_b[2:3, :], potential)
    z_b = y_b - matmul_split(w_a * rows_a[2:3, :], potential, (1, 1))
    return z_a, z_b


def products_of(z, y, w):
    gram = matmul_split(z, z, (1, 1))
    return gram, matmul_split(jnp.concatenate([y, w], 0), z, (1, 1))


def hats_of(samples, inverse):
    hats = matmul_split(samples, inverse, (1, 1))
    return hats[:S], hats[S:]


def swap_halves(value):
    return pltpu.roll(value, S // 2, 1)


def merge_halves(left, right):
    lane = lax.broadcasted_iota(jnp.int32, left.shape, 1)
    return jnp.where(lane < S // 2, left, right)


def half_hats(samples, rows):
    zero = jnp.zeros_like(rows)
    spread = jnp.concatenate(
        [jnp.concatenate([rows, zero], 1), jnp.concatenate([zero, rows], 1)], 0
    )
    return matmul_split(samples, spread, (1, 1))


def pair_products(z_a, z_b, y_a, y_b, w_a, w_b):
    return products_of(
        *(jnp.concatenate([a, b], 1) for a, b in ((z_a, z_b), (y_a, y_b), (w_a, w_b)))
    )


def tree_kernel(
    leaf_count,
    coords_hbm,
    density_hbm,
    probe_ref,
    sketch_ref,
    basis_out,
    top_out,
    probe_win,
    sketch_win,
    z_ref,
    basis_ref,
    coords_ref,
    density_ref,
    points_ref,
    window_ref,
    window_cols,
    halo_xy,
    halo_w,
    high_ref,
    low_ref,
    level_refs,
    gathered,
    rows_mine,
    rows_other,
    mine_ref,
    other_ref,
    hats_ref,
    leaf_inverse,
    work_ref,
    probe_sem,
    sketch_sem,
    out_sem,
    edge_sem,
    point_sem,
    point_out_sem,
    gather_sem,
    send_sem,
    recv_sem,
    basis_sem,
    basis_out_sem,
    load_sem,
):
    span = NODES_PER_CELL
    ranks, leaves = lax.axis_size("rep"), lax.axis_size("leaf")
    rank, position = lax.axis_index("rep"), lax.axis_index("leaf")
    columns, width = probe_ref.shape
    total_leaves = width // span
    chunk = leaf_count * span
    local_levels = leaf_count.bit_length() - 1
    rep_levels = LEAF_LEVELS - local_levels
    merges = rep_levels + CROSS
    family = 1 << CROSS
    mesh_id = pl.DeviceIdType.MESH
    after = lax.rem(position + 1, leaves)
    before = lax.rem(position + leaves - 1, leaves)
    loads = [
        pltpu.make_async_copy(coords_hbm, coords_ref, load_sem.at[0]),
        pltpu.make_async_copy(density_hbm, density_ref, load_sem.at[1]),
    ]
    for load in loads:
        load.start()
    barrier = pltpu.get_barrier_semaphore()

    def signal(leaf, rep):
        pl.semaphore_signal(barrier, inc=1, device_id=(leaf, rep), device_id_type=mesh_id)

    @pl.when(rank == 0)
    def _():
        for k in range(ranks):
            signal(before, k)

    @pl.when(rank == ranks - 1)
    def _():
        for k in range(ranks):
            signal(after, k)

    signal(after, rank)
    signal(before, rank)
    for j in range(1, family):
        signal(position ^ j, rank)
    for k in range(1, ranks):
        signal(position, rank ^ k)
    pl.semaphore_wait(barrier, 2 + 2 + (family - 1) + (ranks - 1))

    def remote(src, dst, sent, arrived, leaf, rep):
        return pltpu.make_async_remote_copy(
            src_ref=src,
            dst_ref=dst,
            send_sem=sent,
            recv_sem=arrived,
            device_id=(leaf, rep),
            device_id_type=mesh_id,
        )

    point_copies = []
    for side, leaf, start in ((0, after, width - span), (1, before, 0)):
        for i, (src, dst) in enumerate(((coords_hbm, halo_xy), (density_hbm, halo_w))):
            point_copies.append(
                remote(
                    src.at[:, pl.ds(start, span)],
                    dst.at[side],
                    point_out_sem.at[2 * side + i],
                    point_sem.at[2 * side + i],
                    leaf,
                    rank,
                )
            )
    for copy in point_copies:
        copy.start()

    own_rows = pl.ds(pl.multiple_of(rank * columns, 8), columns)

    def probe_copy(k, piece, local):
        rep = rank ^ k
        index = rep * leaf_count + piece - 1
        leaf, source = position, index
        if piece == 0:
            leaf = jnp.where(rep == 0, after, position)
            source = jnp.where(rep == 0, total_leaves - 1, index)
        elif piece == leaf_count + 1:
            leaf = jnp.where(rep == ranks - 1, before, position)
            source = jnp.where(rep == ranks - 1, 0, index)
        src = probe_ref.at[:, pl.ds(pl.multiple_of(source * span, span), span)]
        dst = probe_win.at[own_rows, pl.ds(piece * span, span)]
        if local:
            return pltpu.make_async_copy(src, dst, probe_sem.at[piece])
        sent = out_sem.at[k] if k else edge_sem.at[0 if piece == 0 else 1]
        return remote(src, dst, sent, probe_sem.at[piece], leaf, rep)

    def sketch_copy(k, piece):
        rep = rank ^ k
        source = pl.multiple_of((rep * leaf_count + piece) * span, span)
        src = sketch_ref.at[:, pl.ds(source, span)]
        dst = sketch_win.at[own_rows, pl.ds(piece * span, span)]
        if k == 0:
            return pltpu.make_async_copy(src, dst, sketch_sem.at[piece])
        return remote(src, dst, out_sem.at[k], sketch_sem.at[piece], position, rep)

    def start_probe(piece):
        for k in range(1, ranks):
            probe_copy(k, piece, False).start()
        if piece == 0 or piece == leaf_count + 1:
            edge = rank == (0 if piece == 0 else ranks - 1)

            @pl.when(edge)
            def _():
                probe_copy(0, piece, False).start()

            @pl.when(jnp.logical_not(edge))
            def _():
                probe_copy(0, piece, True).start()

        else:
            probe_copy(0, piece, True).start()

    def start_sketch(piece):
        for k in range(1, ranks):
            sketch_copy(k, piece).start()
        sketch_copy(0, piece).start()

    batch = 1
    sent_pieces = 0
    for first in range(0, leaf_count, batch):
        while sent_pieces < first + batch + 2:
            start_probe(sent_pieces)
            sent_pieces += 1
        for piece in range(first, first + batch):
            start_sketch(piece)

    for load in loads:
        load.wait()
    points_ref[...] = jnp.zeros_like(points_ref)
    points_ref[0:2, :] = coords_ref[...]
    points_ref[2:3, :] = density_ref[...]
    blocks = [points_ref[:, t * span : (t + 1) * span] for t in range(total_leaves)]
    nodes = select_lanes(jnp.concatenate(blocks, 0), span // S)
    level_refs[0] = nodes
    for level in range(1, LEAF_LEVELS + 1):
        count = total_leaves >> level
        joined = [
            jnp.concatenate([nodes[16 * i : 16 * i + 8], nodes[16 * i + 8 : 16 * i + 16]], 1)
            for i in range(count)
        ]
        nodes = select_lanes(jnp.concatenate(joined, 0), 2)
        level_refs[level, : 8 * count] = nodes
    place = lax.rem(position, family)
    gathered[place] = nodes

    def gather_copy(j):
        return remote(
            gathered.at[place],
            gathered.at[place],
            gather_sem.at[0],
            gather_sem.at[1],
            position ^ j,
            rank,
        )

    for j in range(1, family):
        gather_copy(j).start()

    def skeleton(level, node):
        rows = level_refs[level, pl.ds(pl.multiple_of(node * 8, 8), 8), :]
        scaled = lax.broadcasted_iota(jnp.int32, rows.shape, 0) == 2
        return jnp.where(scaled, rows * ((span // S) << level), rows)

    for level in range(rep_levels):
        node = rank >> level
        rows_mine[level] = skeleton(local_levels + level, node)
        rows_other[level] = skeleton(local_levels + level, node ^ 1)

    for copy in point_copies:
        copy.wait()
    base = rank * chunk
    window_ref[:, span : span + chunk] = points_ref[:, pl.ds(pl.multiple_of(base, span), chunk)]
    for side in range(2):
        at = 0 if side == 0 else span + chunk
        edge = rank == (0 if side == 0 else ranks - 1)
        inner = base - span if side == 0 else base + chunk
        inner = jnp.where(edge, 0, inner)
        own = points_ref[:, pl.ds(pl.multiple_of(inner, span), span)]
        window_ref[:, at : at + span] = own
        window_ref[0:2, at : at + span] = jnp.where(edge, halo_xy[side], own[0:2])
        window_ref[2:3, at : at + span] = jnp.where(edge, halo_w[side], own[2:3])
    for t in range(leaf_count + 2):
        window_cols[t * span : (t + 1) * span, :] = window_ref[:, t * span : (t + 1) * span].T

    def fill(i, carry):
        own = i > leaf_count
        source = jnp.where(own, i - leaf_count, i)
        target = jnp.where(own, i - leaf_count, i + 1)
        cols = window_cols[pl.ds(pl.multiple_of(source * span, span), span), :]
        rows = window_ref[:, pl.ds(pl.multiple_of(target * span, span), span)]
        delta_x = cols[:, 0:1] - rows[0:1, :]
        delta_y = cols[:, 1:2] - rows[1:2, :]
        squared = delta_x * delta_x + delta_y * delta_y
        same = lax.broadcasted_iota(jnp.int32, (span, span), 0) == lax.broadcasted_iota(
            jnp.int32, (span, span), 1
        )
        squared = jnp.where(same & own, 1.0, squared)
        high, low = split_bf16(jnp.log(squared))
        high_ref[i] = high
        low_ref[i] = low
        return carry

    lax.fori_loop(0, 2 * leaf_count + 1, fill, 0)

    for copy_of in range(1):
        seven = gathered.at[pl.ds(0, family - 1)]
        pltpu.make_async_copy(seven, seven, gather_sem.at[1]).wait()
        pltpu.make_async_copy(seven, seven, gather_sem.at[0]).wait()
    for level in range(CROSS):
        lanes = S >> level
        node = place >> level
        for target_ref, which in ((rows_mine, node), (rows_other, node ^ 1)):
            members = [gathered[(which << level) + m] for m in range(1 << level)]
            if level:
                members = [select_lanes(member, 1 << level) for member in members]
                rows = jnp.concatenate([member[:, :lanes] for member in members], 1)
            else:
                rows = members[0]
            scaled = lax.broadcasted_iota(jnp.int32, rows.shape, 0) == 2
            target_ref[rep_levels + level] = jnp.where(
                scaled, rows * ((span // S) << (LEAF_LEVELS + level)), rows
            )

    def leaf_lanes(t):
        return pl.ds(pl.multiple_of(t * span, span), span)

    def wait_piece(win, sem, piece):
        block = win.at[:, leaf_lanes(piece)]
        pltpu.make_async_copy(block, block, sem.at[piece]).wait()

    def near_of(t):
        weight = window_ref[2:3, leaf_lanes(t + 1)]
        self_term = (1.0 - jnp.log(0.5 * weight)) * (0.5 / math.pi)
        total = probe_win[:, leaf_lanes(t + 1)] * (self_term * weight)
        for offset, block, side in ((0, t, 0), (1, leaf_count + 1 + t, 0), (2, t + 1, 1)):
            scale = window_ref[2:3, leaf_lanes(t + offset)] * LOG_SCALE
            a_high, a_low = split_bf16(probe_win[:, leaf_lanes(t + offset)] * scale)
            b_high, b_low = high_ref[block], low_ref[block]
            for a, b in ((a_high, b_high), (a_high, b_low), (a_low, b_high)):
                total = total + lax.dot_general(
                    a, b, (((1,), (side,)), ((), ())), preferred_element_type=jnp.float32
                )
        return total

    def half(index, carry):
        first = index * batch
        products = []

        @pl.when(index == 0)
        def _():
            wait_piece(probe_win, probe_sem, 0)
            wait_piece(probe_win, probe_sem, 1)

        nears = []
        for i in range(batch):
            wait_piece(probe_win, probe_sem, first + i + 2)
        for i in range(batch):
            nears.append(near_of(first + i))
        for i in range(batch):
            t = first + i
            wait_piece(sketch_win, sketch_sem, t)
            y = sketch_win[:, leaf_lanes(t)]
            z = y - nears[i]
            z_ref[:, leaf_lanes(t)] = z
            w = probe_win[:, leaf_lanes(t + 1)]
            products.append(products_of(z, y, w))
        inverse_factor([p[0] for p in products], work_ref)
        for i, p in enumerate(products):
            leaf_inverse[first + i] = work_ref[i]
            hats_ref[first + i, 0], hats_ref[first + i, 1] = hats_of(p[1], work_ref[i])
        return carry

    def exchange_copy(level, part, stride):
        return remote(
            mine_ref.at[level, part],
            other_ref.at[level, part],
            send_sem.at[level, part],
            recv_sem.at[level, part],
            *peer_of(stride),
        )

    def finish(gram, samples, level, stride):
        stacked = jnp.concatenate([samples[:S], samples[S:]], 1)
        middle = S // 2

        def store(part):
            rows = work_ref[0, part * middle : (part + 1) * middle, :]
            mine_ref[level, part] = half_hats(stacked, rows)

        hooks = {
            middle // 8 - 1: lambda: store(0),
            middle // 8 + SEND_AFTER: lambda: exchange_copy(level, 0, stride).start(),
        }
        inverse_factor([gram], work_ref, hooks)
        store(1)
        exchange_copy(level, 1, stride).start()

    lax.fori_loop(0, leaf_count // batch, half, 0)
    hats = [(hats_ref[i, 0], hats_ref[i, 1]) for i in range(leaf_count)]
    for level in range(local_levels):
        products = []
        for a in range(0, len(hats), 2):
            node = rank * len(hats) + a
            (y_a, w_a), (y_b, w_b) = hats[a], hats[a + 1]
            z_a, z_b = off_diagonal(
                y_a, y_b, w_a, w_b, skeleton(level, node), skeleton(level, node + 1)
            )
            products.append(pair_products(z_a, z_b, y_a, y_b, w_a, w_b))
        if len(products) == 1:
            finish(*products[0], 0, 1)
        else:
            inverse_factor([p[0] for p in products], work_ref)
            hats = [hats_of(p[1], work_ref[t]) for t, p in enumerate(products)]
    if local_levels == 0:
        y, w = hats[0]
        mine_ref[0, 0] = merge_halves(y, swap_halves(w))
        mine_ref[0, 1] = merge_halves(swap_halves(y), w)
        exchange_copy(0, 0, 1).start()
        exchange_copy(0, 1, 1).start()

    def basis_copy(k):
        rep = rank ^ k
        src = basis_ref.at[pl.ds(pl.multiple_of(rep * columns, 8), columns), :]
        dst = basis_out.at[:, pl.ds(pl.multiple_of(rank * chunk, span), chunk)]
        if k == 0:
            return pltpu.make_async_copy(src, dst, basis_sem.at[0])
        return remote(src, dst, basis_out_sem.at[k], basis_sem.at[k], position, rep)

    def exchange(level, stride):
        @pl.when(level == 0)
        def _():
            for t in range(leaf_count):
                at = slice(t * span, (t + 1) * span)
                basis_ref[:, at] = matmul_split(leaf_inverse[t], z_ref[:, at]) * math.sqrt(span)

        @pl.when(level == rep_levels)
        def _():
            for k in range(1, ranks):
                basis_copy(k).start()
            basis_copy(0).start()

        rows_m, rows_o = rows_mine[level], rows_other[level]
        cols_o = rows_o.T
        potential = log_kernel(cols_o, rows_m)
        scaled = potential * cols_o[:, 2:3]
        middle = S // 2
        zero = jnp.zeros((middle, S), jnp.float32)
        top, low = mine_ref[level, 0], mine_ref[level, 1]
        y_m, w_m = merge_halves(top, swap_halves(low)), merge_halves(swap_halves(top), low)
        near_o = matmul_split(w_m * rows_m[2:3, :], potential, (1, 1))
        exchange_copy(level, 0, stride).wait()
        top = other_ref[level, 0]
        z_m = y_m - matmul_split(top, jnp.concatenate([zero, scaled[:middle]], 0))
        exchange_copy(level, 1, stride).wait()
        low = other_ref[level, 1]
        z_m = z_m - matmul_split(low, jnp.concatenate([zero, scaled[middle:]], 0))
        y_o, w_o = merge_halves(top, swap_halves(low)), merge_halves(swap_halves(top), low)
        return z_m, y_o - near_o, y_m, y_o, w_m, w_o

    def step(level, stride):
        gram, samples = pair_products(*exchange(level, stride))
        finish(gram, samples, level + 1, stride * 2)
        return stride * 2

    stride = lax.fori_loop(0, merges - 1, step, 1)
    z_m, z_o = exchange(merges - 1, stride)[:2]
    both = jnp.concatenate([z_m, z_o], 1)
    gram = matmul_split(both, both, (1, 1))
    inverse_factor([gram], work_ref)
    factor = work_ref[0, own_rows, :] * math.sqrt(2 * S)
    second = lax.rem(position // (1 << (CROSS - 1)), 2) == 1
    top_out[:, :S] = matmul_split(factor, jnp.where(second, z_o, z_m))
    top_out[:, S:] = matmul_split(factor, jnp.where(second, z_m, z_o))

    for k in range(ranks):
        basis_copy(k).wait()
    all_sent = probe_ref.at[:, pl.ds(0, (2 * leaf_count + 2) * span)]
    for k in range(1, ranks):
        pltpu.make_async_copy(all_sent, all_sent, out_sem.at[k]).wait()

    @pl.when(rank == 0)
    def _():
        probe_copy(0, 0, False).wait_send()

    @pl.when(rank == ranks - 1)
    def _():
        probe_copy(0, leaf_count + 1, False).wait_send()


def body(curve_coordinates, weighted_density, random_test_matrix, sketch_matrix):
    span = NODES_PER_CELL
    columns, width = random_test_matrix.shape
    ranks = lax.axis_size("rep")
    leaf_count = width // span // ranks
    chunk = leaf_count * span
    merges = LEAF_LEVELS + CROSS - (leaf_count.bit_length() - 1)
    family = 1 << CROSS
    vmem = pl.BlockSpec(memory_space=pltpu.VMEM)
    hbm = pl.BlockSpec(memory_space=pl.ANY)
    f32, bf16 = jnp.float32, jnp.bfloat16
    dma = pltpu.SemaphoreType.DMA
    basis, top = pl.pallas_call(
        functools.partial(tree_kernel, leaf_count),
        out_shape=(
            pltpu.VMEM((columns, width), f32),
            jax.ShapeDtypeStruct((columns, 2 * S), f32),
        ),
        in_specs=[hbm, hbm, hbm, hbm],
        out_specs=(vmem, vmem),
        scratch_shapes=[
            pltpu.VMEM((S, chunk + 2 * span), f32),
            pltpu.VMEM((S, chunk), f32),
            pltpu.VMEM((S, chunk), f32),
            pltpu.VMEM((S, chunk), f32),
            pltpu.VMEM((2, width), f32),
            pltpu.VMEM((1, width), f32),
            pltpu.VMEM((8, width), f32),
            pltpu.VMEM((8, chunk + 2 * span), f32),
            pltpu.VMEM((chunk + 2 * span, 8), f32),
            pltpu.VMEM((2, 2, span), f32),
            pltpu.VMEM((2, 1, span), f32),
            pltpu.VMEM((2 * leaf_count + 1, span, span), bf16),
            pltpu.VMEM((2 * leaf_count + 1, span, span), bf16),
            pltpu.VMEM((LEAF_LEVELS + 1, 8 * (width // span), S), f32),
            pltpu.VMEM((family, 8, S), f32),
            pltpu.VMEM((merges, 8, S), f32),
            pltpu.VMEM((merges, 8, S), f32),
            pltpu.VMEM((merges, 2, S, S), f32),
            pltpu.VMEM((merges, 2, S, S), f32),
            pltpu.VMEM((leaf_count, 2, S, S), f32),
            pltpu.VMEM((leaf_count, S, S), f32),
            pltpu.VMEM((max(2, leaf_count // 2), S, S), f32),
            dma((leaf_count + 2,)),
            dma((leaf_count,)),
            dma((ranks,)),
            dma((2,)),
            dma((4,)),
            dma((4,)),
            dma((2,)),
            dma((merges, 2)),
            dma((merges, 2)),
            dma((ranks,)),
            dma((ranks,)),
            dma((2,)),
        ],
        compiler_params=pltpu.CompilerParams(
            collective_id=0, has_side_effects=True, vmem_limit_bytes=VMEM_LIMIT
        ),
        name="tree",
    )(curve_coordinates, weighted_density[None, :], random_test_matrix, sketch_matrix)
    return (basis, top[None])


def solution(mesh):
    return jax.shard_map(
        body,
        mesh=mesh,
        in_specs=(P(None, "leaf"), P("leaf"), P("rep", "leaf"), P("rep", "leaf")),
        out_specs=(P("rep", "leaf"), P("leaf", "rep", None)),
        check_vma=False,
    )
```

```python
import functools
import math

import jax
import jax.numpy as jnp
from jax import lax
from jax.experimental import pallas as pl
from jax.experimental.pallas import tpu as pltpu
from jax.sharding import PartitionSpec as P

NODES_PER_CELL = 512
S = 128
LEAF_LEVELS = 4
CROSS = 3
NEAR_TILES = (3, 1)
SEND_AFTER = 2
PARTS = ((0, 64), (64, 32), (96, 32))
HIGHEST = lax.Precision.HIGHEST
LOG_SCALE = -0.25 / math.pi
VMEM_LIMIT = 60000 * 1024


def matmul(a, b, contract=(1, 0)):
    return lax.dot_general(
        a,
        b,
        (((contract[0],), (contract[1],)), ((), ())),
        precision=HIGHEST,
        preferred_element_type=jnp.float32,
    )


def split_bf16(value):
    high = value.astype(jnp.bfloat16)
    return high, (value - high.astype(jnp.float32)).astype(jnp.bfloat16)


def matmul_split(a, b, contract=(1, 0)):
    a_high, a_low = split_bf16(a)
    b_high, b_low = split_bf16(b)

    def dot(x, y):
        return lax.dot_general(
            x,
            y,
            (((contract[0],), (contract[1],)), ((), ())),
            preferred_element_type=jnp.float32,
        )

    return dot(a_high, b_high) + (dot(a_high, b_low) + dot(a_low, b_high))


def lane_cast(value, k):
    return jnp.take_along_axis(value, jnp.full(value.shape, k, jnp.int32), axis=1)


def row_cast(value, j):
    return jnp.broadcast_to(value[j : j + 1, :], (8, value.shape[1]))


def eliminate(own, col, following, k, lane, sub):
    at = [sub == j for j in range(8)]
    in_group = (lane >= k) & (lane < k + 8)
    rows = jnp.where(in_group, jnp.where(lane == sub + k, 1.0, 0.0), own)
    out = rows
    pivots = rows
    if following is not None:
        side = [lane_cast(following, k + l) for l in range(8)]
        ahead = [lane_cast(following, k + 8 + l) for l in range(8)]
        following = jnp.where(in_group, 0.0, following)
    for j in range(0, 8, 2):
        both = at[j] | at[j + 1]
        a, b = row_cast(col[j], j), row_cast(col[j], j + 1)
        c = row_cast(col[j + 1], j + 1)
        det = a * c - b * b
        r, inverse_a = 1.0 / det, 1.0 / a
        first, second = row_cast(rows, j), row_cast(rows, j + 1)
        scale_0 = jnp.where(at[j + 1], -b, col[j + 1] * b - col[j] * c)
        scale_0 = jnp.where(at[j], c, scale_0) * r
        scale_1 = jnp.where(at[j + 1], a, col[j] * b - col[j + 1] * a)
        scale_1 = jnp.where(at[j], -b, scale_1) * r
        out = jnp.where(at[j + 1], second - (b * inverse_a) * first, out)
        out = jnp.where(at[j], first, out)
        pivots = jnp.where(at[j], a, jnp.where(at[j + 1], det * inverse_a, pivots))
        rows = (jnp.where(both, 0.0, rows) + scale_0 * first) + scale_1 * second
        if following is not None:
            side_0 = (side[j] * c - side[j + 1] * b) * r
            side_1 = (side[j + 1] * a - side[j] * b) * r
            following = following - side_0 * first - side_1 * second
            for q in range(8):
                left, right = row_cast(side[j], q), row_cast(side[j + 1], q)
                ahead[q] = ahead[q] - side_0 * left - side_1 * right
        for q in range(j + 2, 8):
            above, below = row_cast(col[q], j), row_cast(col[q], j + 1)
            if following is not None:
                side[q] = side[q] - side_0 * above - side_1 * below
            col[q] = (jnp.where(both, 0.0, col[q]) + scale_0 * above) + scale_1 * below
    root = lax.rsqrt(pivots)
    root = root * (1.5 - 0.5 * pivots * root * root)
    result = jnp.where(lane > sub + k, 0.0, out * root)
    return rows, result, following, ahead if following is not None else None


def inverse_factor(grams, work_ref, hooks={}):
    order = grams[0].shape[0]
    count = order // 8
    alone = len(grams) == 1
    near = NEAR_TILES[0 if alone else 1]
    lane = lax.broadcasted_iota(jnp.int32, (8, order), 1)
    sub = lax.broadcasted_iota(jnp.int32, (8, order), 0)
    tiles = [[gram[8 * v : 8 * v + 8, :] for v in range(count)] for gram in grams]
    columns = [None for _ in grams]
    for g in range(count):
        k = 8 * g
        far = g + 1 + near
        in_group = (lane >= k) & (lane < k + 8)
        for i, tile in enumerate(tiles):
            own = tile[g]
            col = columns[i]
            if col is None:
                col = [lane_cast(own, k + l) for l in range(8)]
            following = tile[g + 1] if alone and g + 1 < count else None
            rows, result, following, columns[i] = eliminate(own, col, following, k, lane, sub)
            work_ref[i, k : k + 8, :] = result
            if following is not None:
                tile[g + 1] = following
            solved = [row_cast(rows, j) for j in range(8)]
            for v in range(g + 2 if alone else g + 1, min(far, count)):
                raw = tile[v]
                terms = [lane_cast(raw, k + j) * solved[j] for j in range(8)]
                while len(terms) > 1:
                    terms = [a + b for a, b in zip(terms[::2], terms[1::2])]
                tile[v] = jnp.where(in_group, 0.0, raw) - terms[0]
            if far < count:
                update = matmul(own.T[8 * far :, :], rows)
                for v in range(far, count):
                    kept = jnp.where(in_group, 0.0, tile[v])
                    tile[v] = kept - update[8 * (v - far) : 8 * (v - far) + 8, :]
        if g in hooks:
            hooks[g]()


def peer_of(stride):
    ranks = lax.axis_size("rep")
    place = lax.axis_index("leaf") * ranks + lax.axis_index("rep")
    peer = place + stride * (1 - 2 * ((place // stride) % 2))
    return (peer // ranks, peer % ranks)


def select_lanes(block, stride):
    source = block.shape[1]
    target = source // stride
    take = lax.broadcasted_iota(jnp.int32, (source, target), 0) == stride * lax.broadcasted_iota(
        jnp.int32, (source, target), 1
    )
    return matmul(block, jnp.where(take, 1.0, 0.0))


def log_kernel(source_cols, target_rows):
    delta_x = source_cols[:, 0:1] - target_rows[0:1, :]
    delta_y = source_cols[:, 1:2] - target_rows[1:2, :]
    return jnp.log(delta_x * delta_x + delta_y * delta_y) * LOG_SCALE


def products_of(z, y, w):
    gram = matmul_split(z, z, (1, 1))
    return gram, matmul_split(z, jnp.concatenate([y, w], 0), (1, 1))


def pair_products(z_a, z_b, hats_a, hats_b):
    z = jnp.concatenate([z_a.T, z_b.T], 1)
    gram = matmul_split(z, jnp.concatenate([z_a, z_b], 0))
    return gram, matmul_split(z, jnp.concatenate([hats_a, hats_b], 0))


def coupling(rows_a, rows_b):
    return log_kernel(rows_a.T, rows_b) * rows_b[2:3, :]


def join(hats_a, hats_b, rows_a, rows_b):
    z_a = hats_a[:, :S] - matmul_split(coupling(rows_a, rows_b), hats_b[:, S:])
    z_b = hats_b[:, :S] - matmul_split(coupling(rows_b, rows_a), hats_a[:, S:])
    return pair_products(z_a, z_b, hats_a, hats_b)


def tree_kernel(
    leaf_count,
    coords_hbm,
    density_hbm,
    probe_ref,
    sketch_ref,
    basis_out,
    top_out,
    probe_win,
    sketch_win,
    z_ref,
    basis_ref,
    coords_ref,
    density_ref,
    points_ref,
    window_ref,
    window_cols,
    halo_xy,
    halo_w,
    high_ref,
    low_ref,
    level_refs,
    gathered,
    rows_mine,
    rows_other,
    mine_ref,
    other_ref,
    hats_ref,
    leaf_inverse,
    work_ref,
    probe_sem,
    sketch_sem,
    out_sem,
    edge_sem,
    point_sem,
    point_out_sem,
    gather_sem,
    send_sem,
    recv_sem,
    basis_sem,
    basis_out_sem,
    load_sem,
):
    span = NODES_PER_CELL
    ranks, leaves = lax.axis_size("rep"), lax.axis_size("leaf")
    rank, position = lax.axis_index("rep"), lax.axis_index("leaf")
    columns, width = probe_ref.shape
    total_leaves = width // span
    chunk = leaf_count * span
    local_levels = leaf_count.bit_length() - 1
    rep_levels = LEAF_LEVELS - local_levels
    merges = rep_levels + CROSS
    family = 1 << CROSS
    mesh_id = pl.DeviceIdType.MESH
    after = lax.rem(position + 1, leaves)
    before = lax.rem(position + leaves - 1, leaves)
    loads = [
        pltpu.make_async_copy(coords_hbm, coords_ref, load_sem.at[0]),
        pltpu.make_async_copy(density_hbm, density_ref, load_sem.at[1]),
    ]
    for load in loads:
        load.start()
    barrier = pltpu.get_barrier_semaphore()

    def signal(leaf, rep):
        pl.semaphore_signal(barrier, inc=1, device_id=(leaf, rep), device_id_type=mesh_id)

    @pl.when(rank == 0)
    def _():
        for k in range(ranks):
            signal(before, k)

    @pl.when(rank == ranks - 1)
    def _():
        for k in range(ranks):
            signal(after, k)

    signal(after, rank)
    signal(before, rank)
    for j in range(1, family):
        signal(position ^ j, rank)
    for k in range(1, ranks):
        signal(position, rank ^ k)
    pl.semaphore_wait(barrier, 2 + 2 + (family - 1) + (ranks - 1))

    def remote(src, dst, sent, arrived, leaf, rep):
        return pltpu.make_async_remote_copy(
            src_ref=src,
            dst_ref=dst,
            send_sem=sent,
            recv_sem=arrived,
            device_id=(leaf, rep),
            device_id_type=mesh_id,
        )

    point_copies = []
    for side, leaf, start in ((0, after, width - span), (1, before, 0)):
        for i, (src, dst) in enumerate(((coords_hbm, halo_xy), (density_hbm, halo_w))):
            point_copies.append(
                remote(
                    src.at[:, pl.ds(start, span)],
                    dst.at[side],
                    point_out_sem.at[2 * side + i],
                    point_sem.at[2 * side + i],
                    leaf,
                    rank,
                )
            )
    for copy in point_copies:
        copy.start()

    own_rows = pl.ds(pl.multiple_of(rank * columns, 8), columns)

    def probe_copy(k, piece, local):
        rep = rank ^ k
        index = rep * leaf_count + piece - 1
        leaf, source = position, index
        if piece == 0:
            leaf = jnp.where(rep == 0, after, position)
            source = jnp.where(rep == 0, total_leaves - 1, index)
        elif piece == leaf_count + 1:
            leaf = jnp.where(rep == ranks - 1, before, position)
            source = jnp.where(rep == ranks - 1, 0, index)
        src = probe_ref.at[:, pl.ds(pl.multiple_of(source * span, span), span)]
        dst = probe_win.at[own_rows, pl.ds(piece * span, span)]
        if local:
            return pltpu.make_async_copy(src, dst, probe_sem.at[piece])
        sent = out_sem.at[k] if k else edge_sem.at[0 if piece == 0 else 1]
        return remote(src, dst, sent, probe_sem.at[piece], leaf, rep)

    def sketch_copy(k, piece):
        rep = rank ^ k
        source = pl.multiple_of((rep * leaf_count + piece) * span, span)
        src = sketch_ref.at[:, pl.ds(source, span)]
        dst = sketch_win.at[own_rows, pl.ds(piece * span, span)]
        if k == 0:
            return pltpu.make_async_copy(src, dst, sketch_sem.at[piece])
        return remote(src, dst, out_sem.at[k], sketch_sem.at[piece], position, rep)

    def start_probe(piece):
        for k in range(1, ranks):
            probe_copy(k, piece, False).start()
        if piece == 0 or piece == leaf_count + 1:
            edge = rank == (0 if piece == 0 else ranks - 1)

            @pl.when(edge)
            def _():
                probe_copy(0, piece, False).start()

            @pl.when(jnp.logical_not(edge))
            def _():
                probe_copy(0, piece, True).start()

        else:
            probe_copy(0, piece, True).start()

    def start_sketch(piece):
        for k in range(1, ranks):
            sketch_copy(k, piece).start()
        sketch_copy(0, piece).start()

    batch = 1
    sent_pieces = 0
    for first in range(0, leaf_count, batch):
        while sent_pieces < first + batch + 2:
            start_probe(sent_pieces)
            sent_pieces += 1
        for piece in range(first, first + batch):
            start_sketch(piece)

    for load in loads:
        load.wait()
    points_ref[...] = jnp.zeros_like(points_ref)
    points_ref[0:2, :] = coords_ref[...]
    points_ref[2:3, :] = density_ref[...]
    blocks = [points_ref[:, t * span : (t + 1) * span] for t in range(total_leaves)]
    nodes = select_lanes(jnp.concatenate(blocks, 0), span // S)
    level_refs[0] = nodes
    for level in range(1, LEAF_LEVELS + 1):
        count = total_leaves >> level
        joined = [
            jnp.concatenate([nodes[16 * i : 16 * i + 8], nodes[16 * i + 8 : 16 * i + 16]], 1)
            for i in range(count)
        ]
        nodes = select_lanes(jnp.concatenate(joined, 0), 2)
        level_refs[level, : 8 * count] = nodes
    place = lax.rem(position, family)
    gathered[place] = nodes

    def gather_copy(j):
        return remote(
            gathered.at[place],
            gathered.at[place],
            gather_sem.at[0],
            gather_sem.at[1],
            position ^ j,
            rank,
        )

    for j in range(1, family):
        gather_copy(j).start()

    def skeleton(level, node):
        rows = level_refs[level, pl.ds(pl.multiple_of(node * 8, 8), 8), :]
        scaled = lax.broadcasted_iota(jnp.int32, rows.shape, 0) == 2
        return jnp.where(scaled, rows * ((span // S) << level), rows)

    for level in range(rep_levels):
        node = rank >> level
        rows_mine[level] = skeleton(local_levels + level, node)
        rows_other[level] = skeleton(local_levels + level, node ^ 1)

    for copy in point_copies:
        copy.wait()
    base = rank * chunk
    window_ref[:, span : span + chunk] = points_ref[:, pl.ds(pl.multiple_of(base, span), chunk)]
    for side in range(2):
        at = 0 if side == 0 else span + chunk
        edge = rank == (0 if side == 0 else ranks - 1)
        inner = base - span if side == 0 else base + chunk
        inner = jnp.where(edge, 0, inner)
        own = points_ref[:, pl.ds(pl.multiple_of(inner, span), span)]
        window_ref[:, at : at + span] = own
        window_ref[0:2, at : at + span] = jnp.where(edge, halo_xy[side], own[0:2])
        window_ref[2:3, at : at + span] = jnp.where(edge, halo_w[side], own[2:3])
    for t in range(leaf_count + 2):
        window_cols[t * span : (t + 1) * span, :] = window_ref[:, t * span : (t + 1) * span].T

    def fill(i, carry):
        own = i > leaf_count
        source = jnp.where(own, i - leaf_count, i)
        target = jnp.where(own, i - leaf_count, i + 1)
        cols = window_cols[pl.ds(pl.multiple_of(source * span, span), span), :]
        rows = window_ref[:, pl.ds(pl.multiple_of(target * span, span), span)]
        delta_x = cols[:, 0:1] - rows[0:1, :]
        delta_y = cols[:, 1:2] - rows[1:2, :]
        squared = delta_x * delta_x + delta_y * delta_y
        same = lax.broadcasted_iota(jnp.int32, (span, span), 0) == lax.broadcasted_iota(
            jnp.int32, (span, span), 1
        )
        squared = jnp.where(same & own, 1.0, squared)
        high, low = split_bf16(jnp.log(squared))
        high_ref[i] = high
        low_ref[i] = low
        return carry

    lax.fori_loop(0, 2 * leaf_count + 1, fill, 0)

    for copy_of in range(1):
        seven = gathered.at[pl.ds(0, family - 1)]
        pltpu.make_async_copy(seven, seven, gather_sem.at[1]).wait()
        pltpu.make_async_copy(seven, seven, gather_sem.at[0]).wait()
    for level in range(CROSS):
        lanes = S >> level
        node = place >> level
        for target_ref, which in ((rows_mine, node), (rows_other, node ^ 1)):
            members = [gathered[(which << level) + m] for m in range(1 << level)]
            if level:
                members = [select_lanes(member, 1 << level) for member in members]
                rows = jnp.concatenate([member[:, :lanes] for member in members], 1)
            else:
                rows = members[0]
            scaled = lax.broadcasted_iota(jnp.int32, rows.shape, 0) == 2
            target_ref[rep_levels + level] = jnp.where(
                scaled, rows * ((span // S) << (LEAF_LEVELS + level)), rows
            )

    def leaf_lanes(t):
        return pl.ds(pl.multiple_of(t * span, span), span)

    def wait_piece(win, sem, piece):
        block = win.at[:, leaf_lanes(piece)]
        pltpu.make_async_copy(block, block, sem.at[piece]).wait()

    def near_of(t):
        weight = window_ref[2:3, leaf_lanes(t + 1)]
        self_term = (1.0 - jnp.log(0.5 * weight)) * (0.5 / math.pi)
        total = probe_win[:, leaf_lanes(t + 1)] * (self_term * weight)
        for offset, block, side in ((0, t, 0), (1, leaf_count + 1 + t, 0), (2, t + 1, 1)):
            scale = window_ref[2:3, leaf_lanes(t + offset)] * LOG_SCALE
            a_high, a_low = split_bf16(probe_win[:, leaf_lanes(t + offset)] * scale)
            b_high, b_low = high_ref[block], low_ref[block]
            for a, b in ((a_high, b_high), (a_high, b_low), (a_low, b_high)):
                total = total + lax.dot_general(
                    a, b, (((1,), (side,)), ((), ())), preferred_element_type=jnp.float32
                )
        return total

    def half(index, carry):
        first = index * batch
        products = []

        @pl.when(index == 0)
        def _():
            wait_piece(probe_win, probe_sem, 0)
            wait_piece(probe_win, probe_sem, 1)

        nears = []
        for i in range(batch):
            wait_piece(probe_win, probe_sem, first + i + 2)
        for i in range(batch):
            nears.append(near_of(first + i))
        for i in range(batch):
            t = first + i
            wait_piece(sketch_win, sketch_sem, t)
            y = sketch_win[:, leaf_lanes(t)]
            z = y - nears[i]
            z_ref[:, leaf_lanes(t)] = z
            w = probe_win[:, leaf_lanes(t + 1)]
            products.append(products_of(z, y, w))
        inverse_factor([p[0] for p in products], work_ref)
        for i, p in enumerate(products):
            leaf_inverse[first + i] = work_ref[i]
            hats_ref[first + i] = matmul_split(work_ref[i], p[1])
        return carry

    def exchange_copy(level, part, stride):
        rows = pl.ds(*PARTS[part])
        return remote(
            mine_ref.at[level, rows],
            other_ref.at[level, rows],
            send_sem.at[level, part],
            recv_sem.at[level, part],
            *peer_of(stride),
        )

    def finish(gram, samples, level, stride):
        def store(part):
            rows = slice(PARTS[part][0], sum(PARTS[part]))
            mine_ref[level, rows] = matmul_split(work_ref[0, rows, :], samples)

        def send(part):
            exchange_copy(level, part, stride).start()

        hooks = {}
        for part in range(len(PARTS) - 1):
            ready = sum(PARTS[part]) // 8 - 1
            hooks[ready] = functools.partial(store, part)
            hooks[ready + SEND_AFTER] = functools.partial(send, part)
        inverse_factor([gram], work_ref, hooks)
        store(len(PARTS) - 1)
        send(len(PARTS) - 1)

    lax.fori_loop(0, leaf_count // batch, half, 0)
    hats = [hats_ref[i] for i in range(leaf_count)]
    for level in range(local_levels):
        products = []
        for a in range(0, len(hats), 2):
            node = rank * len(hats) + a
            products.append(
                join(hats[a], hats[a + 1], skeleton(level, node), skeleton(level, node + 1))
            )
        if len(products) == 1:
            finish(*products[0], 0, 1)
        else:
            inverse_factor([p[0] for p in products], work_ref)
            hats = [matmul_split(work_ref[t], p[1]) for t, p in enumerate(products)]
    if local_levels == 0:
        mine_ref[0] = hats[0]
        for part in range(len(PARTS)):
            exchange_copy(0, part, 1).start()

    def basis_copy(k):
        rep = rank ^ k
        src = basis_ref.at[pl.ds(pl.multiple_of(rep * columns, 8), columns), :]
        dst = basis_out.at[:, pl.ds(pl.multiple_of(rank * chunk, span), chunk)]
        if k == 0:
            return pltpu.make_async_copy(src, dst, basis_sem.at[0])
        return remote(src, dst, basis_out_sem.at[k], basis_sem.at[k], position, rep)

    def exchange(level, stride):
        share = max(1, leaf_count // 2) if rep_levels else leaf_count

        @pl.when(level * share < leaf_count)
        def _():
            for i in range(share):
                t = level * share + i
                part = matmul_split(leaf_inverse[t], z_ref[:, leaf_lanes(t)])
                basis_ref[:, leaf_lanes(t)] = part * math.sqrt(span)

        @pl.when(level == rep_levels)
        def _():
            for k in range(1, ranks):
                basis_copy(k).start()
            basis_copy(0).start()

        rows_m, rows_o = rows_mine[level], rows_other[level]
        to_mine, to_other = coupling(rows_m, rows_o), coupling(rows_o, rows_m)
        hats_m = mine_ref[level]
        z_m = hats_m[:, :S]
        near_o = matmul_split(to_other, hats_m[:, S:])
        for part, (start, size) in enumerate(PARTS):
            exchange_copy(level, part, stride).wait()
            rows = [other_ref[level, start : start + size, S:]]
            if start:
                rows.insert(0, jnp.zeros((start, S), jnp.float32))
            if start + size < S:
                rows.append(jnp.zeros((S - start - size, S), jnp.float32))
            z_m = z_m - matmul_split(to_mine, jnp.concatenate(rows, 0))
        hats_o = other_ref[level]
        return z_m, hats_o[:, :S] - near_o, hats_m, hats_o

    def step(level, stride):
        gram, samples = pair_products(*exchange(level, stride))
        finish(gram, samples, level + 1, stride * 2)
        return stride * 2

    stride = lax.fori_loop(0, merges - 1, step, 1)
    z_m, z_o = exchange(merges - 1, stride)[:2]
    stacked = jnp.concatenate([z_m, z_o], 0)
    z_m, z_o = z_m.T, z_o.T
    gram = matmul_split(jnp.concatenate([z_m, z_o], 1), stacked)
    inverse_factor([gram], work_ref)
    factor = work_ref[0, own_rows, :] * math.sqrt(2 * S)
    second = lax.rem(position // (1 << (CROSS - 1)), 2) == 1
    top_out[:, :S] = matmul_split(factor, jnp.where(second, z_o, z_m))
    top_out[:, S:] = matmul_split(factor, jnp.where(second, z_m, z_o))

    for k in range(ranks):
        basis_copy(k).wait()
    all_sent = probe_ref.at[:, pl.ds(0, (2 * leaf_count + 2) * span)]
    for k in range(1, ranks):
        pltpu.make_async_copy(all_sent, all_sent, out_sem.at[k]).wait()

    @pl.when(rank == 0)
    def _():
        probe_copy(0, 0, False).wait_send()

    @pl.when(rank == ranks - 1)
    def _():
        probe_copy(0, leaf_count + 1, False).wait_send()


def body(curve_coordinates, weighted_density, random_test_matrix, sketch_matrix):
    span = NODES_PER_CELL
    columns, width = random_test_matrix.shape
    ranks = lax.axis_size("rep")
    leaf_count = width // span // ranks
    chunk = leaf_count * span
    merges = LEAF_LEVELS + CROSS - (leaf_count.bit_length() - 1)
    family = 1 << CROSS
    vmem = pl.BlockSpec(memory_space=pltpu.VMEM)
    hbm = pl.BlockSpec(memory_space=pl.ANY)
    f32, bf16 = jnp.float32, jnp.bfloat16
    dma = pltpu.SemaphoreType.DMA
    basis, top = pl.pallas_call(
        functools.partial(tree_kernel, leaf_count),
        out_shape=(
            pltpu.VMEM((columns, width), f32),
            pltpu.VMEM((columns, 2 * S), f32),
        ),
        in_specs=[hbm, hbm, hbm, hbm],
        out_specs=(vmem, vmem),
        scratch_shapes=[
            pltpu.VMEM((S, chunk + 2 * span), f32),
            pltpu.VMEM((S, chunk), f32),
            pltpu.VMEM((S, chunk), f32),
            pltpu.VMEM((S, chunk), f32),
            pltpu.VMEM((2, width), f32),
            pltpu.VMEM((1, width), f32),
            pltpu.VMEM((8, width), f32),
            pltpu.VMEM((8, chunk + 2 * span), f32),
            pltpu.VMEM((chunk + 2 * span, 8), f32),
            pltpu.VMEM((2, 2, span), f32),
            pltpu.VMEM((2, 1, span), f32),
            pltpu.VMEM((2 * leaf_count + 1, span, span), bf16),
            pltpu.VMEM((2 * leaf_count + 1, span, span), bf16),
            pltpu.VMEM((LEAF_LEVELS + 1, 8 * (width // span), S), f32),
            pltpu.VMEM((family, 8, S), f32),
            pltpu.VMEM((merges, 8, S), f32),
            pltpu.VMEM((merges, 8, S), f32),
            pltpu.VMEM((merges, S, 2 * S), f32),
            pltpu.VMEM((merges, S, 2 * S), f32),
            pltpu.VMEM((leaf_count, S, 2 * S), f32),
            pltpu.VMEM((leaf_count, S, S), f32),
            pltpu.VMEM((max(2, leaf_count // 2), S, S), f32),
            dma((leaf_count + 2,)),
            dma((leaf_count,)),
            dma((ranks,)),
            dma((2,)),
            dma((4,)),
            dma((4,)),
            dma((2,)),
            dma((merges, len(PARTS))),
            dma((merges, len(PARTS))),
            dma((ranks,)),
            dma((ranks,)),
            dma((2,)),
        ],
        compiler_params=pltpu.CompilerParams(
            collective_id=0, has_side_effects=True, vmem_limit_bytes=VMEM_LIMIT
        ),
        name="tree",
    )(curve_coordinates, weighted_density[None, :], random_test_matrix, sketch_matrix)
    return (basis, top[None])


def solution(mesh):
    return jax.shard_map(
        body,
        mesh=mesh,
        in_specs=(P(None, "leaf"), P("leaf"), P("rep", "leaf"), P("rep", "leaf")),
        out_specs=(P("rep", "leaf"), P("leaf", "rep", None)),
        check_vma=False,
    )
```

```python
import functools
import math

import jax
import jax.numpy as jnp
from jax import lax
from jax.experimental import pallas as pl
from jax.experimental.pallas import tpu as pltpu
from jax.sharding import PartitionSpec as P

NODES_PER_CELL = 512
S = 128
LEAF_LEVELS = 4
CROSS = 3
NEAR_TILES = (3, 1)
SEND_AFTER = 1
PARTS = ((0, 64), (64, 32), (96, 32))
HIGHEST = lax.Precision.HIGHEST
LOG_SCALE = -0.25 / math.pi
VMEM_LIMIT = 60000 * 1024


def matmul(a, b, contract=(1, 0)):
    return lax.dot_general(
        a,
        b,
        (((contract[0],), (contract[1],)), ((), ())),
        precision=HIGHEST,
        preferred_element_type=jnp.float32,
    )


def split_bf16(value):
    high = value.astype(jnp.bfloat16)
    return high, (value - high.astype(jnp.float32)).astype(jnp.bfloat16)


def matmul_split(a, b, contract=(1, 0)):
    a_high, a_low = split_bf16(a)
    b_high, b_low = split_bf16(b)

    def dot(x, y):
        return lax.dot_general(
            x,
            y,
            (((contract[0],), (contract[1],)), ((), ())),
            preferred_element_type=jnp.float32,
        )

    return dot(a_high, b_high) + (dot(a_high, b_low) + dot(a_low, b_high))


def lane_cast(value, k):
    return jnp.take_along_axis(value, jnp.full(value.shape, k, jnp.int32), axis=1)


def row_cast(value, j):
    return jnp.broadcast_to(value[j : j + 1, :], (8, value.shape[1]))


def eliminate(own, col, following, k, lane, sub):
    at = [sub == j for j in range(8)]
    in_group = (lane >= k) & (lane < k + 8)
    rows = jnp.where(in_group, jnp.where(lane == sub + k, 1.0, 0.0), own)
    out = rows
    pivots = rows
    if following is not None:
        side = [lane_cast(following, k + l) for l in range(8)]
        ahead = [lane_cast(following, k + 8 + l) for l in range(8)]
        following = jnp.where(in_group, 0.0, following)
    for j in range(0, 8, 2):
        both = at[j] | at[j + 1]
        a, b = row_cast(col[j], j), row_cast(col[j], j + 1)
        c = row_cast(col[j + 1], j + 1)
        det = a * c - b * b
        r, inverse_a = 1.0 / det, 1.0 / a
        first, second = row_cast(rows, j), row_cast(rows, j + 1)
        scale_0 = jnp.where(at[j + 1], -b, col[j + 1] * b - col[j] * c)
        scale_0 = jnp.where(at[j], c, scale_0) * r
        scale_1 = jnp.where(at[j + 1], a, col[j] * b - col[j + 1] * a)
        scale_1 = jnp.where(at[j], -b, scale_1) * r
        out = jnp.where(at[j + 1], second - (b * inverse_a) * first, out)
        out = jnp.where(at[j], first, out)
        pivots = jnp.where(at[j], a, jnp.where(at[j + 1], det * inverse_a, pivots))
        rows = (jnp.where(both, 0.0, rows) + scale_0 * first) + scale_1 * second
        if following is not None:
            side_0 = (side[j] * c - side[j + 1] * b) * r
            side_1 = (side[j + 1] * a - side[j] * b) * r
            following = following - side_0 * first - side_1 * second
            for q in range(8):
                left, right = row_cast(side[j], q), row_cast(side[j + 1], q)
                ahead[q] = ahead[q] - side_0 * left - side_1 * right
        for q in range(j + 2, 8):
            above, below = row_cast(col[q], j), row_cast(col[q], j + 1)
            if following is not None:
                side[q] = side[q] - side_0 * above - side_1 * below
            col[q] = (jnp.where(both, 0.0, col[q]) + scale_0 * above) + scale_1 * below
    root = lax.rsqrt(pivots)
    root = root * (1.5 - 0.5 * pivots * root * root)
    result = jnp.where(lane > sub + k, 0.0, out * root)
    return rows, result, following, ahead if following is not None else None


def inverse_factor(grams, work_ref, hooks={}):
    order = grams[0].shape[0]
    count = order // 8
    alone = len(grams) == 1
    near = NEAR_TILES[0 if alone else 1]
    lane = lax.broadcasted_iota(jnp.int32, (8, order), 1)
    sub = lax.broadcasted_iota(jnp.int32, (8, order), 0)
    tiles = [[gram[8 * v : 8 * v + 8, :] for v in range(count)] for gram in grams]
    columns = [None for _ in grams]
    for g in range(count):
        k = 8 * g
        far = g + 1 + near
        in_group = (lane >= k) & (lane < k + 8)
        for i, tile in enumerate(tiles):
            own = tile[g]
            col = columns[i]
            if col is None:
                col = [lane_cast(own, k + l) for l in range(8)]
            following = tile[g + 1] if alone and g + 1 < count else None
            rows, result, following, columns[i] = eliminate(own, col, following, k, lane, sub)
            work_ref[i, k : k + 8, :] = result
            if following is not None:
                tile[g + 1] = following
            solved = [row_cast(rows, j) for j in range(8)]
            for v in range(g + 2 if alone else g + 1, min(far, count)):
                raw = tile[v]
                terms = [lane_cast(raw, k + j) * solved[j] for j in range(8)]
                while len(terms) > 1:
                    terms = [a + b for a, b in zip(terms[::2], terms[1::2])]
                tile[v] = jnp.where(in_group, 0.0, raw) - terms[0]
            if far < count:
                update = matmul_split(own.T[8 * far :, :], rows)
                for v in range(far, count):
                    kept = jnp.where(in_group, 0.0, tile[v])
                    tile[v] = kept - update[8 * (v - far) : 8 * (v - far) + 8, :]
        if g in hooks:
            hooks[g]()


def peer_of(stride):
    ranks = lax.axis_size("rep")
    place = lax.axis_index("leaf") * ranks + lax.axis_index("rep")
    peer = place + stride * (1 - 2 * ((place // stride) % 2))
    return (peer // ranks, peer % ranks)


def select_lanes(block, stride):
    source = block.shape[1]
    target = source // stride
    take = lax.broadcasted_iota(jnp.int32, (source, target), 0) == stride * lax.broadcasted_iota(
        jnp.int32, (source, target), 1
    )
    return matmul(block, jnp.where(take, 1.0, 0.0))


def log_kernel(source_cols, target_rows):
    delta_x = source_cols[:, 0:1] - target_rows[0:1, :]
    delta_y = source_cols[:, 1:2] - target_rows[1:2, :]
    return jnp.log(delta_x * delta_x + delta_y * delta_y) * LOG_SCALE


def products_of(z, y, w):
    gram = matmul_split(z, z, (1, 1))
    return gram, matmul_split(z, jnp.concatenate([y, w], 0), (1, 1))


def pair_products(z_a, z_b, hats_a, hats_b):
    z = jnp.concatenate([z_a.T, z_b.T], 1)
    gram = matmul_split(z, jnp.concatenate([z_a, z_b], 0))
    return gram, matmul_split(z, jnp.concatenate([hats_a, hats_b], 0))


def coupling(rows_a, rows_b):
    return log_kernel(rows_a.T, rows_b) * rows_b[2:3, :]


def join(hats_a, hats_b, rows_a, rows_b):
    z_a = hats_a[:, :S] - matmul_split(coupling(rows_a, rows_b), hats_b[:, S:])
    z_b = hats_b[:, :S] - matmul_split(coupling(rows_b, rows_a), hats_a[:, S:])
    return pair_products(z_a, z_b, hats_a, hats_b)


def tree_kernel(
    leaf_count,
    coords_hbm,
    density_hbm,
    probe_ref,
    sketch_ref,
    basis_out,
    top_out,
    probe_win,
    sketch_win,
    z_ref,
    basis_ref,
    coords_ref,
    density_ref,
    points_ref,
    window_ref,
    window_cols,
    halo_xy,
    halo_w,
    high_ref,
    low_ref,
    level_refs,
    gathered,
    rows_mine,
    rows_other,
    mine_ref,
    other_ref,
    hats_ref,
    leaf_inverse,
    work_ref,
    probe_sem,
    sketch_sem,
    out_sem,
    edge_sem,
    point_sem,
    point_out_sem,
    gather_sem,
    send_sem,
    recv_sem,
    basis_sem,
    basis_out_sem,
    load_sem,
):
    span = NODES_PER_CELL
    ranks, leaves = lax.axis_size("rep"), lax.axis_size("leaf")
    rank, position = lax.axis_index("rep"), lax.axis_index("leaf")
    columns, width = probe_ref.shape
    total_leaves = width // span
    chunk = leaf_count * span
    local_levels = leaf_count.bit_length() - 1
    rep_levels = LEAF_LEVELS - local_levels
    merges = rep_levels + CROSS
    family = 1 << CROSS
    mesh_id = pl.DeviceIdType.MESH
    after = lax.rem(position + 1, leaves)
    before = lax.rem(position + leaves - 1, leaves)
    loads = [
        pltpu.make_async_copy(coords_hbm, coords_ref, load_sem.at[0]),
        pltpu.make_async_copy(density_hbm, density_ref, load_sem.at[1]),
    ]
    for load in loads:
        load.start()
    barrier = pltpu.get_barrier_semaphore()

    def signal(leaf, rep):
        pl.semaphore_signal(barrier, inc=1, device_id=(leaf, rep), device_id_type=mesh_id)

    @pl.when(rank == 0)
    def _():
        for k in range(ranks):
            signal(before, k)

    @pl.when(rank == ranks - 1)
    def _():
        for k in range(ranks):
            signal(after, k)

    signal(after, rank)
    signal(before, rank)
    for j in range(1, family):
        signal(position ^ j, rank)
    for k in range(1, ranks):
        signal(position, rank ^ k)
    pl.semaphore_wait(barrier, 2 + 2 + (family - 1) + (ranks - 1))

    def remote(src, dst, sent, arrived, leaf, rep):
        return pltpu.make_async_remote_copy(
            src_ref=src,
            dst_ref=dst,
            send_sem=sent,
            recv_sem=arrived,
            device_id=(leaf, rep),
            device_id_type=mesh_id,
        )

    point_copies = []
    for side, leaf, start in ((0, after, width - span), (1, before, 0)):
        for i, (src, dst) in enumerate(((coords_hbm, halo_xy), (density_hbm, halo_w))):
            point_copies.append(
                remote(
                    src.at[:, pl.ds(start, span)],
                    dst.at[side],
                    point_out_sem.at[2 * side + i],
                    point_sem.at[2 * side + i],
                    leaf,
                    rank,
                )
            )
    for copy in point_copies:
        copy.start()

    own_rows = pl.ds(pl.multiple_of(rank * columns, 8), columns)

    def probe_copy(k, piece, local):
        rep = rank ^ k
        index = rep * leaf_count + piece - 1
        leaf, source = position, index
        if piece == 0:
            leaf = jnp.where(rep == 0, after, position)
            source = jnp.where(rep == 0, total_leaves - 1, index)
        elif piece == leaf_count + 1:
            leaf = jnp.where(rep == ranks - 1, before, position)
            source = jnp.where(rep == ranks - 1, 0, index)
        src = probe_ref.at[:, pl.ds(pl.multiple_of(source * span, span), span)]
        dst = probe_win.at[own_rows, pl.ds(piece * span, span)]
        if local:
            return pltpu.make_async_copy(src, dst, probe_sem.at[piece])
        sent = out_sem.at[k] if k else edge_sem.at[0 if piece == 0 else 1]
        return remote(src, dst, sent, probe_sem.at[piece], leaf, rep)

    def sketch_copy(k, piece):
        rep = rank ^ k
        source = pl.multiple_of((rep * leaf_count + piece) * span, span)
        src = sketch_ref.at[:, pl.ds(source, span)]
        dst = sketch_win.at[own_rows, pl.ds(piece * span, span)]
        if k == 0:
            return pltpu.make_async_copy(src, dst, sketch_sem.at[piece])
        return remote(src, dst, out_sem.at[k], sketch_sem.at[piece], position, rep)

    def start_probe(piece):
        for k in range(1, ranks):
            probe_copy(k, piece, False).start()
        if piece == 0 or piece == leaf_count + 1:
            edge = rank == (0 if piece == 0 else ranks - 1)

            @pl.when(edge)
            def _():
                probe_copy(0, piece, False).start()

            @pl.when(jnp.logical_not(edge))
            def _():
                probe_copy(0, piece, True).start()

        else:
            probe_copy(0, piece, True).start()

    def start_sketch(piece):
        for k in range(1, ranks):
            sketch_copy(k, piece).start()
        sketch_copy(0, piece).start()

    batch = 1
    sent_pieces = 0
    for first in range(0, leaf_count, batch):
        while sent_pieces < first + batch + 2:
            start_probe(sent_pieces)
            sent_pieces += 1
        for piece in range(first, first + batch):
            start_sketch(piece)

    for load in loads:
        load.wait()
    points_ref[...] = jnp.zeros_like(points_ref)
    points_ref[0:2, :] = coords_ref[...]
    points_ref[2:3, :] = density_ref[...]
    blocks = [points_ref[:, t * span : (t + 1) * span] for t in range(total_leaves)]
    nodes = select_lanes(jnp.concatenate(blocks, 0), span // S)
    level_refs[0] = nodes
    for level in range(1, LEAF_LEVELS + 1):
        count = total_leaves >> level
        joined = [
            jnp.concatenate([nodes[16 * i : 16 * i + 8], nodes[16 * i + 8 : 16 * i + 16]], 1)
            for i in range(count)
        ]
        nodes = select_lanes(jnp.concatenate(joined, 0), 2)
        level_refs[level, : 8 * count] = nodes
    place = lax.rem(position, family)
    gathered[place] = nodes

    def gather_copy(j):
        return remote(
            gathered.at[place],
            gathered.at[place],
            gather_sem.at[0],
            gather_sem.at[1],
            position ^ j,
            rank,
        )

    for j in range(1, family):
        gather_copy(j).start()

    def skeleton(level, node):
        rows = level_refs[level, pl.ds(pl.multiple_of(node * 8, 8), 8), :]
        scaled = lax.broadcasted_iota(jnp.int32, rows.shape, 0) == 2
        return jnp.where(scaled, rows * ((span // S) << level), rows)

    for level in range(rep_levels):
        node = rank >> level
        rows_mine[level] = skeleton(local_levels + level, node)
        rows_other[level] = skeleton(local_levels + level, node ^ 1)

    for copy in point_copies:
        copy.wait()
    base = rank * chunk
    window_ref[:, span : span + chunk] = points_ref[:, pl.ds(pl.multiple_of(base, span), chunk)]
    for side in range(2):
        at = 0 if side == 0 else span + chunk
        edge = rank == (0 if side == 0 else ranks - 1)
        inner = base - span if side == 0 else base + chunk
        inner = jnp.where(edge, 0, inner)
        own = points_ref[:, pl.ds(pl.multiple_of(inner, span), span)]
        window_ref[:, at : at + span] = own
        window_ref[0:2, at : at + span] = jnp.where(edge, halo_xy[side], own[0:2])
        window_ref[2:3, at : at + span] = jnp.where(edge, halo_w[side], own[2:3])
    for t in range(leaf_count + 2):
        window_cols[t * span : (t + 1) * span, :] = window_ref[:, t * span : (t + 1) * span].T

    def fill(i, carry):
        own = i > leaf_count
        source = jnp.where(own, i - leaf_count, i)
        target = jnp.where(own, i - leaf_count, i + 1)
        cols = window_cols[pl.ds(pl.multiple_of(source * span, span), span), :]
        rows = window_ref[:, pl.ds(pl.multiple_of(target * span, span), span)]
        delta_x = cols[:, 0:1] - rows[0:1, :]
        delta_y = cols[:, 1:2] - rows[1:2, :]
        squared = delta_x * delta_x + delta_y * delta_y
        same = lax.broadcasted_iota(jnp.int32, (span, span), 0) == lax.broadcasted_iota(
            jnp.int32, (span, span), 1
        )
        squared = jnp.where(same & own, 1.0, squared)
        high, low = split_bf16(jnp.log(squared))
        high_ref[i] = high
        low_ref[i] = low
        return carry

    lax.fori_loop(0, 2 * leaf_count + 1, fill, 0)

    for copy_of in range(1):
        seven = gathered.at[pl.ds(0, family - 1)]
        pltpu.make_async_copy(seven, seven, gather_sem.at[1]).wait()
        pltpu.make_async_copy(seven, seven, gather_sem.at[0]).wait()
    for level in range(CROSS):
        lanes = S >> level
        node = place >> level
        for target_ref, which in ((rows_mine, node), (rows_other, node ^ 1)):
            members = [gathered[(which << level) + m] for m in range(1 << level)]
            if level:
                members = [select_lanes(member, 1 << level) for member in members]
                rows = jnp.concatenate([member[:, :lanes] for member in members], 1)
            else:
                rows = members[0]
            scaled = lax.broadcasted_iota(jnp.int32, rows.shape, 0) == 2
            target_ref[rep_levels + level] = jnp.where(
                scaled, rows * ((span // S) << (LEAF_LEVELS + level)), rows
            )

    def leaf_lanes(t):
        return pl.ds(pl.multiple_of(t * span, span), span)

    def wait_piece(win, sem, piece):
        block = win.at[:, leaf_lanes(piece)]
        pltpu.make_async_copy(block, block, sem.at[piece]).wait()

    def near_of(t):
        weight = window_ref[2:3, leaf_lanes(t + 1)]
        self_term = (1.0 - jnp.log(0.5 * weight)) * (0.5 / math.pi)
        total = probe_win[:, leaf_lanes(t + 1)] * (self_term * weight)
        for offset, block, side in ((0, t, 0), (1, leaf_count + 1 + t, 0), (2, t + 1, 1)):
            scale = window_ref[2:3, leaf_lanes(t + offset)] * LOG_SCALE
            a_high, a_low = split_bf16(probe_win[:, leaf_lanes(t + offset)] * scale)
            b_high, b_low = high_ref[block], low_ref[block]
            for a, b in ((a_high, b_high), (a_high, b_low), (a_low, b_high)):
                total = total + lax.dot_general(
                    a, b, (((1,), (side,)), ((), ())), preferred_element_type=jnp.float32
                )
        return total

    def half(index, carry):
        first = index * batch
        products = []

        @pl.when(index == 0)
        def _():
            wait_piece(probe_win, probe_sem, 0)
            wait_piece(probe_win, probe_sem, 1)

        nears = []
        for i in range(batch):
            wait_piece(probe_win, probe_sem, first + i + 2)
        for i in range(batch):
            nears.append(near_of(first + i))
        for i in range(batch):
            t = first + i
            wait_piece(sketch_win, sketch_sem, t)
            y = sketch_win[:, leaf_lanes(t)]
            z = y - nears[i]
            z_ref[:, leaf_lanes(t)] = z
            w = probe_win[:, leaf_lanes(t + 1)]
            products.append(products_of(z, y, w))
        inverse_factor([p[0] for p in products], work_ref)
        for i, p in enumerate(products):
            leaf_inverse[first + i] = work_ref[i]
            hats_ref[first + i] = matmul_split(work_ref[i], p[1])
        return carry

    def exchange_copy(level, part, stride):
        rows = pl.ds(*PARTS[part])
        return remote(
            mine_ref.at[level, rows],
            other_ref.at[level, rows],
            send_sem.at[level, part],
            recv_sem.at[level, part],
            *peer_of(stride),
        )

    def finish(gram, samples, level, stride):
        def store(part):
            rows = slice(PARTS[part][0], sum(PARTS[part]))
            mine_ref[level, rows] = matmul_split(work_ref[0, rows, :], samples)

        def send(part):
            exchange_copy(level, part, stride).start()

        hooks = {}
        for part in range(len(PARTS) - 1):
            ready = sum(PARTS[part]) // 8 - 1
            hooks[ready] = functools.partial(store, part)
            hooks[ready + SEND_AFTER] = functools.partial(send, part)
        inverse_factor([gram], work_ref, hooks)
        store(len(PARTS) - 1)
        send(len(PARTS) - 1)

    lax.fori_loop(0, leaf_count // batch, half, 0)
    hats = [hats_ref[i] for i in range(leaf_count)]
    for level in range(local_levels):
        products = []
        for a in range(0, len(hats), 2):
            node = rank * len(hats) + a
            products.append(
                join(hats[a], hats[a + 1], skeleton(level, node), skeleton(level, node + 1))
            )
        if len(products) == 1:
            finish(*products[0], 0, 1)
        else:
            inverse_factor([p[0] for p in products], work_ref)
            hats = [matmul_split(work_ref[t], p[1]) for t, p in enumerate(products)]
    if local_levels == 0:
        mine_ref[0] = hats[0]
        for part in range(len(PARTS)):
            exchange_copy(0, part, 1).start()

    def basis_copy(k):
        rep = rank ^ k
        src = basis_ref.at[pl.ds(pl.multiple_of(rep * columns, 8), columns), :]
        dst = basis_out.at[:, pl.ds(pl.multiple_of(rank * chunk, span), chunk)]
        if k == 0:
            return pltpu.make_async_copy(src, dst, basis_sem.at[0])
        return remote(src, dst, basis_out_sem.at[k], basis_sem.at[k], position, rep)

    def exchange(level, stride):
        share = max(1, leaf_count // 2) if rep_levels else leaf_count

        @pl.when(level * share < leaf_count)
        def _():
            for i in range(share):
                t = level * share + i
                part = matmul_split(leaf_inverse[t], z_ref[:, leaf_lanes(t)])
                basis_ref[:, leaf_lanes(t)] = part * math.sqrt(span)

        @pl.when(level == rep_levels)
        def _():
            for k in range(1, ranks):
                basis_copy(k).start()
            basis_copy(0).start()

        rows_m, rows_o = rows_mine[level], rows_other[level]
        to_mine, to_other = coupling(rows_m, rows_o), coupling(rows_o, rows_m)
        hats_m = mine_ref[level]
        z_m = hats_m[:, :S]
        near_o = matmul_split(to_other, hats_m[:, S:])
        for part, (start, size) in enumerate(PARTS):
            exchange_copy(level, part, stride).wait()
            rows = [other_ref[level, start : start + size, S:]]
            if start:
                rows.insert(0, jnp.zeros((start, S), jnp.float32))
            if start + size < S:
                rows.append(jnp.zeros((S - start - size, S), jnp.float32))
            z_m = z_m - matmul_split(to_mine, jnp.concatenate(rows, 0))
        hats_o = other_ref[level]
        return z_m, hats_o[:, :S] - near_o, hats_m, hats_o

    def step(level, stride):
        gram, samples = pair_products(*exchange(level, stride))
        finish(gram, samples, level + 1, stride * 2)
        return stride * 2

    stride = lax.fori_loop(0, merges - 1, step, 1)
    z_m, z_o = exchange(merges - 1, stride)[:2]
    stacked = jnp.concatenate([z_m, z_o], 0)
    z_m, z_o = z_m.T, z_o.T
    gram = matmul_split(jnp.concatenate([z_m, z_o], 1), stacked)
    inverse_factor([gram], work_ref)
    factor = work_ref[0, own_rows, :] * math.sqrt(2 * S)
    second = lax.rem(position // (1 << (CROSS - 1)), 2) == 1
    top_out[:, :S] = matmul_split(factor, jnp.where(second, z_o, z_m))
    top_out[:, S:] = matmul_split(factor, jnp.where(second, z_m, z_o))

    for k in range(ranks):
        basis_copy(k).wait()
    all_sent = probe_ref.at[:, pl.ds(0, (2 * leaf_count + 2) * span)]
    for k in range(1, ranks):
        pltpu.make_async_copy(all_sent, all_sent, out_sem.at[k]).wait()

    @pl.when(rank == 0)
    def _():
        probe_copy(0, 0, False).wait_send()

    @pl.when(rank == ranks - 1)
    def _():
        probe_copy(0, leaf_count + 1, False).wait_send()


def body(curve_coordinates, weighted_density, random_test_matrix, sketch_matrix):
    span = NODES_PER_CELL
    columns, width = random_test_matrix.shape
    ranks = lax.axis_size("rep")
    leaf_count = width // span // ranks
    chunk = leaf_count * span
    merges = LEAF_LEVELS + CROSS - (leaf_count.bit_length() - 1)
    family = 1 << CROSS
    vmem = pl.BlockSpec(memory_space=pltpu.VMEM)
    hbm = pl.BlockSpec(memory_space=pl.ANY)
    f32, bf16 = jnp.float32, jnp.bfloat16
    dma = pltpu.SemaphoreType.DMA
    basis, top = pl.pallas_call(
        functools.partial(tree_kernel, leaf_count),
        out_shape=(
            pltpu.VMEM((columns, width), f32),
            pltpu.VMEM((columns, 2 * S), f32),
        ),
        in_specs=[hbm, hbm, hbm, hbm],
        out_specs=(vmem, vmem),
        scratch_shapes=[
            pltpu.VMEM((S, chunk + 2 * span), f32),
            pltpu.VMEM((S, chunk), f32),
            pltpu.VMEM((S, chunk), f32),
            pltpu.VMEM((S, chunk), f32),
            pltpu.VMEM((2, width), f32),
            pltpu.VMEM((1, width), f32),
            pltpu.VMEM((8, width), f32),
            pltpu.VMEM((8, chunk + 2 * span), f32),
            pltpu.VMEM((chunk + 2 * span, 8), f32),
            pltpu.VMEM((2, 2, span), f32),
            pltpu.VMEM((2, 1, span), f32),
            pltpu.VMEM((2 * leaf_count + 1, span, span), bf16),
            pltpu.VMEM((2 * leaf_count + 1, span, span), bf16),
            pltpu.VMEM((LEAF_LEVELS + 1, 8 * (width // span), S), f32),
            pltpu.VMEM((family, 8, S), f32),
            pltpu.VMEM((merges, 8, S), f32),
            pltpu.VMEM((merges, 8, S), f32),
            pltpu.VMEM((merges, S, 2 * S), f32),
            pltpu.VMEM((merges, S, 2 * S), f32),
            pltpu.VMEM((leaf_count, S, 2 * S), f32),
            pltpu.VMEM((leaf_count, S, S), f32),
            pltpu.VMEM((max(2, leaf_count // 2), S, S), f32),
            dma((leaf_count + 2,)),
            dma((leaf_count,)),
            dma((ranks,)),
            dma((2,)),
            dma((4,)),
            dma((4,)),
            dma((2,)),
            dma((merges, len(PARTS))),
            dma((merges, len(PARTS))),
            dma((ranks,)),
            dma((ranks,)),
            dma((2,)),
        ],
        compiler_params=pltpu.CompilerParams(
            collective_id=0, has_side_effects=True, vmem_limit_bytes=VMEM_LIMIT
        ),
        name="tree",
    )(curve_coordinates, weighted_density[None, :], random_test_matrix, sketch_matrix)
    return (basis, top[None])


def solution(mesh):
    return jax.shard_map(
        body,
        mesh=mesh,
        in_specs=(P(None, "leaf"), P("leaf"), P("rep", "leaf"), P("rep", "leaf")),
        out_specs=(P("rep", "leaf"), P("leaf", "rep", None)),
        check_vma=False,
    )
```

```python
import functools
import math

import jax
import jax.numpy as jnp
from jax import lax
from jax.experimental import pallas as pl
from jax.experimental.pallas import tpu as pltpu
from jax.sharding import PartitionSpec as P

NODES_PER_CELL = 512
S = 128
LEAF_LEVELS = 4
CROSS = 3
NEAR_TILES = (2, 1)
SEND_AFTER = 1
PARTS = ((0, 64), (64, 32), (96, 32))
HIGHEST = lax.Precision.HIGHEST
LOG_SCALE = -0.25 / math.pi
VMEM_LIMIT = 60000 * 1024


def matmul(a, b, contract=(1, 0)):
    return lax.dot_general(
        a,
        b,
        (((contract[0],), (contract[1],)), ((), ())),
        precision=HIGHEST,
        preferred_element_type=jnp.float32,
    )


def split_bf16(value):
    high = value.astype(jnp.bfloat16)
    return high, (value - high.astype(jnp.float32)).astype(jnp.bfloat16)


def matmul_split(a, b, contract=(1, 0)):
    a_high, a_low = split_bf16(a)
    b_high, b_low = split_bf16(b)

    def dot(x, y):
        return lax.dot_general(
            x,
            y,
            (((contract[0],), (contract[1],)), ((), ())),
            preferred_element_type=jnp.float32,
        )

    return dot(a_high, b_high) + (dot(a_high, b_low) + dot(a_low, b_high))


def lane_cast(value, k):
    return jnp.take_along_axis(value, jnp.full(value.shape, k, jnp.int32), axis=1)


def row_cast(value, j):
    return jnp.broadcast_to(value[j : j + 1, :], (8, value.shape[1]))


def eliminate(own, col, following, k, lane, sub):
    at = [sub == j for j in range(8)]
    in_group = (lane >= k) & (lane < k + 8)
    rows = jnp.where(in_group, jnp.where(lane == sub + k, 1.0, 0.0), own)
    out = rows
    pivots = rows
    if following is not None:
        side = [lane_cast(following, k + l) for l in range(8)]
        ahead = [lane_cast(following, k + 8 + l) for l in range(8)]
        following = jnp.where(in_group, 0.0, following)
    for j in range(0, 8, 2):
        both = at[j] | at[j + 1]
        a, b = row_cast(col[j], j), row_cast(col[j], j + 1)
        c = row_cast(col[j + 1], j + 1)
        det = a * c - b * b
        r, inverse_a = 1.0 / det, 1.0 / a
        first, second = row_cast(rows, j), row_cast(rows, j + 1)
        scale_0 = jnp.where(at[j + 1], -b, col[j + 1] * b - col[j] * c)
        scale_0 = jnp.where(at[j], c, scale_0) * r
        scale_1 = jnp.where(at[j + 1], a, col[j] * b - col[j + 1] * a)
        scale_1 = jnp.where(at[j], -b, scale_1) * r
        out = jnp.where(at[j + 1], second - (b * inverse_a) * first, out)
        out = jnp.where(at[j], first, out)
        pivots = jnp.where(at[j], a, jnp.where(at[j + 1], det * inverse_a, pivots))
        rows = (jnp.where(both, 0.0, rows) + scale_0 * first) + scale_1 * second
        if following is not None:
            side_0 = (side[j] * c - side[j + 1] * b) * r
            side_1 = (side[j + 1] * a - side[j] * b) * r
            following = following - side_0 * first - side_1 * second
            for q in range(8):
                left, right = row_cast(side[j], q), row_cast(side[j + 1], q)
                ahead[q] = ahead[q] - side_0 * left - side_1 * right
        for q in range(j + 2, 8):
            above, below = row_cast(col[q], j), row_cast(col[q], j + 1)
            if following is not None:
                side[q] = side[q] - side_0 * above - side_1 * below
            col[q] = (jnp.where(both, 0.0, col[q]) + scale_0 * above) + scale_1 * below
    root = lax.rsqrt(pivots)
    root = root * (1.5 - 0.5 * pivots * root * root)
    result = jnp.where(lane > sub + k, 0.0, out * root)
    return rows, result, following, ahead if following is not None else None


def inverse_factor(grams, work_ref, hooks={}):
    order = grams[0].shape[0]
    count = order // 8
    alone = len(grams) == 1
    near = NEAR_TILES[0 if alone else 1]
    lane = lax.broadcasted_iota(jnp.int32, (8, order), 1)
    sub = lax.broadcasted_iota(jnp.int32, (8, order), 0)
    tiles = [[gram[8 * v : 8 * v + 8, :] for v in range(count)] for gram in grams]
    columns = [None for _ in grams]
    for g in range(count):
        k = 8 * g
        far = g + 1 + near
        in_group = (lane >= k) & (lane < k + 8)
        for i, tile in enumerate(tiles):
            own = tile[g]
            col = columns[i]
            if col is None:
                col = [lane_cast(own, k + l) for l in range(8)]
            following = tile[g + 1] if alone and g + 1 < count else None
            rows, result, following, columns[i] = eliminate(own, col, following, k, lane, sub)
            work_ref[i, k : k + 8, :] = result
            if following is not None:
                tile[g + 1] = following
            solved = [row_cast(rows, j) for j in range(8)]
            for v in range(g + 2 if alone else g + 1, min(far, count)):
                raw = tile[v]
                terms = [lane_cast(raw, k + j) * solved[j] for j in range(8)]
                while len(terms) > 1:
                    terms = [a + b for a, b in zip(terms[::2], terms[1::2])]
                tile[v] = jnp.where(in_group, 0.0, raw) - terms[0]
            if far < count:
                update = matmul_split(own.T[8 * far :, :], rows)
                for v in range(far, count):
                    kept = jnp.where(in_group, 0.0, tile[v])
                    tile[v] = kept - update[8 * (v - far) : 8 * (v - far) + 8, :]
        if g in hooks:
            hooks[g]()


def peer_of(stride):
    ranks = lax.axis_size("rep")
    place = lax.axis_index("leaf") * ranks + lax.axis_index("rep")
    peer = place + stride * (1 - 2 * ((place // stride) % 2))
    return (peer // ranks, peer % ranks)


def select_lanes(block, stride):
    source = block.shape[1]
    target = source // stride
    take = lax.broadcasted_iota(jnp.int32, (source, target), 0) == stride * lax.broadcasted_iota(
        jnp.int32, (source, target), 1
    )
    return matmul(block, jnp.where(take, 1.0, 0.0))


def log_kernel(source_cols, target_rows):
    delta_x = source_cols[:, 0:1] - target_rows[0:1, :]
    delta_y = source_cols[:, 1:2] - target_rows[1:2, :]
    return jnp.log(delta_x * delta_x + delta_y * delta_y) * LOG_SCALE


def products_of(z, y, w):
    gram = matmul_split(z, z, (1, 1))
    return gram, matmul_split(z, jnp.concatenate([y, w], 0), (1, 1))


def pair_products(z_a, z_b, hats_a, hats_b):
    z = jnp.concatenate([z_a.T, z_b.T], 1)
    gram = matmul_split(z, jnp.concatenate([z_a, z_b], 0))
    return gram, matmul_split(z, jnp.concatenate([hats_a, hats_b], 0))


def coupling(rows_a, rows_b):
    return log_kernel(rows_a.T, rows_b) * rows_b[2:3, :]


def join(hats_a, hats_b, rows_a, rows_b):
    z_a = hats_a[:, :S] - matmul_split(coupling(rows_a, rows_b), hats_b[:, S:])
    z_b = hats_b[:, :S] - matmul_split(coupling(rows_b, rows_a), hats_a[:, S:])
    return pair_products(z_a, z_b, hats_a, hats_b)


def tree_kernel(
    leaf_count,
    coords_hbm,
    density_hbm,
    probe_ref,
    sketch_ref,
    basis_out,
    top_out,
    probe_win,
    sketch_win,
    z_ref,
    basis_ref,
    coords_ref,
    density_ref,
    points_ref,
    window_ref,
    window_cols,
    halo_xy,
    halo_w,
    high_ref,
    low_ref,
    level_refs,
    gathered,
    rows_mine,
    rows_other,
    mine_ref,
    other_ref,
    hats_ref,
    leaf_inverse,
    work_ref,
    probe_sem,
    sketch_sem,
    out_sem,
    edge_sem,
    point_sem,
    point_out_sem,
    gather_sem,
    send_sem,
    recv_sem,
    basis_sem,
    basis_out_sem,
    load_sem,
):
    span = NODES_PER_CELL
    ranks, leaves = lax.axis_size("rep"), lax.axis_size("leaf")
    rank, position = lax.axis_index("rep"), lax.axis_index("leaf")
    columns, width = probe_ref.shape
    total_leaves = width // span
    chunk = leaf_count * span
    local_levels = leaf_count.bit_length() - 1
    rep_levels = LEAF_LEVELS - local_levels
    merges = rep_levels + CROSS
    family = 1 << CROSS
    mesh_id = pl.DeviceIdType.MESH
    after = lax.rem(position + 1, leaves)
    before = lax.rem(position + leaves - 1, leaves)
    loads = [
        pltpu.make_async_copy(coords_hbm, coords_ref, load_sem.at[0]),
        pltpu.make_async_copy(density_hbm, density_ref, load_sem.at[1]),
    ]
    for load in loads:
        load.start()
    barrier = pltpu.get_barrier_semaphore()

    def signal(leaf, rep):
        pl.semaphore_signal(barrier, inc=1, device_id=(leaf, rep), device_id_type=mesh_id)

    @pl.when(rank == 0)
    def _():
        for k in range(ranks):
            signal(before, k)

    @pl.when(rank == ranks - 1)
    def _():
        for k in range(ranks):
            signal(after, k)

    signal(after, rank)
    signal(before, rank)
    for j in range(1, family):
        signal(position ^ j, rank)
    for k in range(1, ranks):
        signal(position, rank ^ k)
    pl.semaphore_wait(barrier, 2 + 2 + (family - 1) + (ranks - 1))

    def remote(src, dst, sent, arrived, leaf, rep):
        return pltpu.make_async_remote_copy(
            src_ref=src,
            dst_ref=dst,
            send_sem=sent,
            recv_sem=arrived,
            device_id=(leaf, rep),
            device_id_type=mesh_id,
        )

    point_copies = []
    for side, leaf, start in ((0, after, width - span), (1, before, 0)):
        for i, (src, dst) in enumerate(((coords_hbm, halo_xy), (density_hbm, halo_w))):
            point_copies.append(
                remote(
                    src.at[:, pl.ds(start, span)],
                    dst.at[side],
                    point_out_sem.at[2 * side + i],
                    point_sem.at[2 * side + i],
                    leaf,
                    rank,
                )
            )
    for copy in point_copies:
        copy.start()

    own_rows = pl.ds(pl.multiple_of(rank * columns, 8), columns)

    def probe_copy(k, piece, local):
        rep = rank ^ k
        index = rep * leaf_count + piece - 1
        leaf, source = position, index
        if piece == 0:
            leaf = jnp.where(rep == 0, after, position)
            source = jnp.where(rep == 0, total_leaves - 1, index)
        elif piece == leaf_count + 1:
            leaf = jnp.where(rep == ranks - 1, before, position)
            source = jnp.where(rep == ranks - 1, 0, index)
        src = probe_ref.at[:, pl.ds(pl.multiple_of(source * span, span), span)]
        dst = probe_win.at[own_rows, pl.ds(piece * span, span)]
        if local:
            return pltpu.make_async_copy(src, dst, probe_sem.at[piece])
        sent = out_sem.at[k] if k else edge_sem.at[0 if piece == 0 else 1]
        return remote(src, dst, sent, probe_sem.at[piece], leaf, rep)

    def sketch_copy(k, piece):
        rep = rank ^ k
        source = pl.multiple_of((rep * leaf_count + piece) * span, span)
        src = sketch_ref.at[:, pl.ds(source, span)]
        dst = sketch_win.at[own_rows, pl.ds(piece * span, span)]
        if k == 0:
            return pltpu.make_async_copy(src, dst, sketch_sem.at[piece])
        return remote(src, dst, out_sem.at[k], sketch_sem.at[piece], position, rep)

    def start_probe(piece):
        for k in range(1, ranks):
            probe_copy(k, piece, False).start()
        if piece == 0 or piece == leaf_count + 1:
            edge = rank == (0 if piece == 0 else ranks - 1)

            @pl.when(edge)
            def _():
                probe_copy(0, piece, False).start()

            @pl.when(jnp.logical_not(edge))
            def _():
                probe_copy(0, piece, True).start()

        else:
            probe_copy(0, piece, True).start()

    def start_sketch(piece):
        for k in range(1, ranks):
            sketch_copy(k, piece).start()
        sketch_copy(0, piece).start()

    batch = 1
    sent_pieces = 0
    for first in range(0, leaf_count, batch):
        while sent_pieces < first + batch + 2:
            start_probe(sent_pieces)
            sent_pieces += 1
        for piece in range(first, first + batch):
            start_sketch(piece)

    for load in loads:
        load.wait()
    points_ref[...] = jnp.zeros_like(points_ref)
    points_ref[0:2, :] = coords_ref[...]
    points_ref[2:3, :] = density_ref[...]
    blocks = [points_ref[:, t * span : (t + 1) * span] for t in range(total_leaves)]
    nodes = select_lanes(jnp.concatenate(blocks, 0), span // S)
    level_refs[0] = nodes
    for level in range(1, LEAF_LEVELS + 1):
        count = total_leaves >> level
        joined = [
            jnp.concatenate([nodes[16 * i : 16 * i + 8], nodes[16 * i + 8 : 16 * i + 16]], 1)
            for i in range(count)
        ]
        nodes = select_lanes(jnp.concatenate(joined, 0), 2)
        level_refs[level, : 8 * count] = nodes
    place = lax.rem(position, family)
    gathered[place] = nodes

    def gather_copy(j):
        return remote(
            gathered.at[place],
            gathered.at[place],
            gather_sem.at[0],
            gather_sem.at[1],
            position ^ j,
            rank,
        )

    for j in range(1, family):
        gather_copy(j).start()

    def skeleton(level, node):
        rows = level_refs[level, pl.ds(pl.multiple_of(node * 8, 8), 8), :]
        scaled = lax.broadcasted_iota(jnp.int32, rows.shape, 0) == 2
        return jnp.where(scaled, rows * ((span // S) << level), rows)

    for level in range(rep_levels):
        node = rank >> level
        rows_mine[level] = skeleton(local_levels + level, node)
        rows_other[level] = skeleton(local_levels + level, node ^ 1)

    for copy in point_copies:
        copy.wait()
    base = rank * chunk
    window_ref[:, span : span + chunk] = points_ref[:, pl.ds(pl.multiple_of(base, span), chunk)]
    for side in range(2):
        at = 0 if side == 0 else span + chunk
        edge = rank == (0 if side == 0 else ranks - 1)
        inner = base - span if side == 0 else base + chunk
        inner = jnp.where(edge, 0, inner)
        own = points_ref[:, pl.ds(pl.multiple_of(inner, span), span)]
        window_ref[:, at : at + span] = own
        window_ref[0:2, at : at + span] = jnp.where(edge, halo_xy[side], own[0:2])
        window_ref[2:3, at : at + span] = jnp.where(edge, halo_w[side], own[2:3])
    for t in range(leaf_count + 2):
        window_cols[t * span : (t + 1) * span, :] = window_ref[:, t * span : (t + 1) * span].T

    def fill(i, carry):
        own = i > leaf_count
        source = jnp.where(own, i - leaf_count, i)
        target = jnp.where(own, i - leaf_count, i + 1)
        cols = window_cols[pl.ds(pl.multiple_of(source * span, span), span), :]
        rows = window_ref[:, pl.ds(pl.multiple_of(target * span, span), span)]
        delta_x = cols[:, 0:1] - rows[0:1, :]
        delta_y = cols[:, 1:2] - rows[1:2, :]
        squared = delta_x * delta_x + delta_y * delta_y
        same = lax.broadcasted_iota(jnp.int32, (span, span), 0) == lax.broadcasted_iota(
            jnp.int32, (span, span), 1
        )
        squared = jnp.where(same & own, 1.0, squared)
        high, low = split_bf16(jnp.log(squared))
        high_ref[i] = high
        low_ref[i] = low
        return carry

    lax.fori_loop(0, 2 * leaf_count + 1, fill, 0)

    for copy_of in range(1):
        seven = gathered.at[pl.ds(0, family - 1)]
        pltpu.make_async_copy(seven, seven, gather_sem.at[1]).wait()
        pltpu.make_async_copy(seven, seven, gather_sem.at[0]).wait()
    for level in range(CROSS):
        lanes = S >> level
        node = place >> level
        for target_ref, which in ((rows_mine, node), (rows_other, node ^ 1)):
            members = [gathered[(which << level) + m] for m in range(1 << level)]
            if level:
                members = [select_lanes(member, 1 << level) for member in members]
                rows = jnp.concatenate([member[:, :lanes] for member in members], 1)
            else:
                rows = members[0]
            scaled = lax.broadcasted_iota(jnp.int32, rows.shape, 0) == 2
            target_ref[rep_levels + level] = jnp.where(
                scaled, rows * ((span // S) << (LEAF_LEVELS + level)), rows
            )

    def leaf_lanes(t):
        return pl.ds(pl.multiple_of(t * span, span), span)

    def wait_piece(win, sem, piece):
        block = win.at[:, leaf_lanes(piece)]
        pltpu.make_async_copy(block, block, sem.at[piece]).wait()

    def near_of(t):
        weight = window_ref[2:3, leaf_lanes(t + 1)]
        self_term = (1.0 - jnp.log(0.5 * weight)) * (0.5 / math.pi)
        total = probe_win[:, leaf_lanes(t + 1)] * (self_term * weight)
        for offset, block, side in ((0, t, 0), (1, leaf_count + 1 + t, 0), (2, t + 1, 1)):
            scale = window_ref[2:3, leaf_lanes(t + offset)] * LOG_SCALE
            a_high, a_low = split_bf16(probe_win[:, leaf_lanes(t + offset)] * scale)
            b_high, b_low = high_ref[block], low_ref[block]
            for a, b in ((a_high, b_high), (a_high, b_low), (a_low, b_high)):
                total = total + lax.dot_general(
                    a, b, (((1,), (side,)), ((), ())), preferred_element_type=jnp.float32
                )
        return total

    def half(index, carry):
        first = index * batch
        products = []

        @pl.when(index == 0)
        def _():
            wait_piece(probe_win, probe_sem, 0)
            wait_piece(probe_win, probe_sem, 1)

        nears = []
        for i in range(batch):
            wait_piece(probe_win, probe_sem, first + i + 2)
        for i in range(batch):
            nears.append(near_of(first + i))
        for i in range(batch):
            t = first + i
            wait_piece(sketch_win, sketch_sem, t)
            y = sketch_win[:, leaf_lanes(t)]
            z = y - nears[i]
            z_ref[:, leaf_lanes(t)] = z
            w = probe_win[:, leaf_lanes(t + 1)]
            products.append(products_of(z, y, w))
        inverse_factor([p[0] for p in products], work_ref)
        for i, p in enumerate(products):
            leaf_inverse[first + i] = work_ref[i]
            hats_ref[first + i] = matmul_split(work_ref[i], p[1])
        return carry

    def exchange_copy(level, part, stride):
        rows = pl.ds(*PARTS[part])
        return remote(
            mine_ref.at[level, rows],
            other_ref.at[level, rows],
            send_sem.at[level, part],
            recv_sem.at[level, part],
            *peer_of(stride),
        )

    def finish(gram, samples, level, stride):
        def store(part):
            rows = slice(PARTS[part][0], sum(PARTS[part]))
            mine_ref[level, rows] = matmul_split(work_ref[0, rows, :], samples)

        def send(part):
            exchange_copy(level, part, stride).start()

        hooks = {}
        for part in range(len(PARTS) - 1):
            ready = sum(PARTS[part]) // 8 - 1
            hooks[ready] = functools.partial(store, part)
            hooks[ready + SEND_AFTER] = functools.partial(send, part)
        inverse_factor([gram], work_ref, hooks)
        store(len(PARTS) - 1)
        send(len(PARTS) - 1)

    lax.fori_loop(0, leaf_count // batch, half, 0)
    hats = [hats_ref[i] for i in range(leaf_count)]
    for level in range(local_levels):
        products = []
        for a in range(0, len(hats), 2):
            node = rank * len(hats) + a
            products.append(
                join(hats[a], hats[a + 1], skeleton(level, node), skeleton(level, node + 1))
            )
        if len(products) == 1:
            finish(*products[0], 0, 1)
        else:
            inverse_factor([p[0] for p in products], work_ref)
            hats = [matmul_split(work_ref[t], p[1]) for t, p in enumerate(products)]
    if local_levels == 0:
        mine_ref[0] = hats[0]
        for part in range(len(PARTS)):
            exchange_copy(0, part, 1).start()

    def basis_copy(k):
        rep = rank ^ k
        src = basis_ref.at[pl.ds(pl.multiple_of(rep * columns, 8), columns), :]
        dst = basis_out.at[:, pl.ds(pl.multiple_of(rank * chunk, span), chunk)]
        if k == 0:
            return pltpu.make_async_copy(src, dst, basis_sem.at[0])
        return remote(src, dst, basis_out_sem.at[k], basis_sem.at[k], position, rep)

    def exchange(level, stride):
        share = max(1, leaf_count // 2) if rep_levels else leaf_count

        @pl.when(level * share < leaf_count)
        def _():
            for i in range(share):
                t = level * share + i
                part = matmul_split(leaf_inverse[t], z_ref[:, leaf_lanes(t)])
                basis_ref[:, leaf_lanes(t)] = part * math.sqrt(span)

        @pl.when(level == rep_levels)
        def _():
            for k in range(1, ranks):
                basis_copy(k).start()
            basis_copy(0).start()

        rows_m, rows_o = rows_mine[level], rows_other[level]
        to_mine, to_other = coupling(rows_m, rows_o), coupling(rows_o, rows_m)
        hats_m = mine_ref[level]
        z_m = hats_m[:, :S]
        near_o = matmul_split(to_other, hats_m[:, S:])
        for part, (start, size) in enumerate(PARTS):
            exchange_copy(level, part, stride).wait()
            rows = [other_ref[level, start : start + size, S:]]
            if start:
                rows.insert(0, jnp.zeros((start, S), jnp.float32))
            if start + size < S:
                rows.append(jnp.zeros((S - start - size, S), jnp.float32))
            z_m = z_m - matmul_split(to_mine, jnp.concatenate(rows, 0))
        hats_o = other_ref[level]
        return z_m, hats_o[:, :S] - near_o, hats_m, hats_o

    def step(level, stride):
        gram, samples = pair_products(*exchange(level, stride))
        finish(gram, samples, level + 1, stride * 2)
        return stride * 2

    stride = lax.fori_loop(0, merges - 1, step, 1)
    z_m, z_o = exchange(merges - 1, stride)[:2]
    stacked = jnp.concatenate([z_m, z_o], 0)
    z_m, z_o = z_m.T, z_o.T
    gram = matmul_split(jnp.concatenate([z_m, z_o], 1), stacked)
    inverse_factor([gram], work_ref)
    factor = work_ref[0, own_rows, :] * math.sqrt(2 * S)
    second = lax.rem(position // (1 << (CROSS - 1)), 2) == 1
    top_out[:, :S] = matmul_split(factor, jnp.where(second, z_o, z_m))
    top_out[:, S:] = matmul_split(factor, jnp.where(second, z_m, z_o))

    for k in range(ranks):
        basis_copy(k).wait()
    all_sent = probe_ref.at[:, pl.ds(0, (2 * leaf_count + 2) * span)]
    for k in range(1, ranks):
        pltpu.make_async_copy(all_sent, all_sent, out_sem.at[k]).wait()

    @pl.when(rank == 0)
    def _():
        probe_copy(0, 0, False).wait_send()

    @pl.when(rank == ranks - 1)
    def _():
        probe_copy(0, leaf_count + 1, False).wait_send()


def body(curve_coordinates, weighted_density, random_test_matrix, sketch_matrix):
    span = NODES_PER_CELL
    columns, width = random_test_matrix.shape
    ranks = lax.axis_size("rep")
    leaf_count = width // span // ranks
    chunk = leaf_count * span
    merges = LEAF_LEVELS + CROSS - (leaf_count.bit_length() - 1)
    family = 1 << CROSS
    vmem = pl.BlockSpec(memory_space=pltpu.VMEM)
    hbm = pl.BlockSpec(memory_space=pl.ANY)
    f32, bf16 = jnp.float32, jnp.bfloat16
    dma = pltpu.SemaphoreType.DMA
    basis, top = pl.pallas_call(
        functools.partial(tree_kernel, leaf_count),
        out_shape=(
            pltpu.VMEM((columns, width), f32),
            pltpu.VMEM((columns, 2 * S), f32),
        ),
        in_specs=[hbm, hbm, hbm, hbm],
        out_specs=(vmem, vmem),
        scratch_shapes=[
            pltpu.VMEM((S, chunk + 2 * span), f32),
            pltpu.VMEM((S, chunk), f32),
            pltpu.VMEM((S, chunk), f32),
            pltpu.VMEM((S, chunk), f32),
            pltpu.VMEM((2, width), f32),
            pltpu.VMEM((1, width), f32),
            pltpu.VMEM((8, width), f32),
            pltpu.VMEM((8, chunk + 2 * span), f32),
            pltpu.VMEM((chunk + 2 * span, 8), f32),
            pltpu.VMEM((2, 2, span), f32),
            pltpu.VMEM((2, 1, span), f32),
            pltpu.VMEM((2 * leaf_count + 1, span, span), bf16),
            pltpu.VMEM((2 * leaf_count + 1, span, span), bf16),
            pltpu.VMEM((LEAF_LEVELS + 1, 8 * (width // span), S), f32),
            pltpu.VMEM((family, 8, S), f32),
            pltpu.VMEM((merges, 8, S), f32),
            pltpu.VMEM((merges, 8, S), f32),
            pltpu.VMEM((merges, S, 2 * S), f32),
            pltpu.VMEM((merges, S, 2 * S), f32),
            pltpu.VMEM((leaf_count, S, 2 * S), f32),
            pltpu.VMEM((leaf_count, S, S), f32),
            pltpu.VMEM((max(2, leaf_count // 2), S, S), f32),
            dma((leaf_count + 2,)),
            dma((leaf_count,)),
            dma((ranks,)),
            dma((2,)),
            dma((4,)),
            dma((4,)),
            dma((2,)),
            dma((merges, len(PARTS))),
            dma((merges, len(PARTS))),
            dma((ranks,)),
            dma((ranks,)),
            dma((2,)),
        ],
        compiler_params=pltpu.CompilerParams(
            collective_id=0, has_side_effects=True, vmem_limit_bytes=VMEM_LIMIT
        ),
        name="tree",
    )(curve_coordinates, weighted_density[None, :], random_test_matrix, sketch_matrix)
    return (basis, top[None])


def solution(mesh):
    return jax.shard_map(
        body,
        mesh=mesh,
        in_specs=(P(None, "leaf"), P("leaf"), P("rep", "leaf"), P("rep", "leaf")),
        out_specs=(P("rep", "leaf"), P("leaf", "rep", None)),
        check_vma=False,
    )
```
